32 devices in a mesh: row: 4 (over y, x), col: 8 (over z, core).
Axes of the slice: x: 2, y: 2, z: 4, core: 2. Of those that a mesh axis runs over, the one named last changes fastest.
Arguments:
- transmission: float32 [2, 1024, 2048], P(None, 'row', 'col'), may hold values from -5 to 5
- probe_modes: float32 [2, 2, 256, 256], replicated, may hold values from -5 to 5
- measured: float32 [64, 256, 256], P(('row', 'col')), may hold values from 0.2 to 8
- offset_down: int32 [64], P(('row', 'col')), may hold values from 0 to 255, as said below
- offset_across: int32 [64], P(('row', 'col')), may hold values from 0 to 255, as said below
Outputs:
- object_gradient: float32 [2, 1024, 2048], P(None, 'row', 'col')
- probe_gradient: float32 [2, 2, 256, 256], replicated
The draws below stay inside these ranges and needn't reach their ends.
Inputs may be any that keep to these rules, and one draw needn't show every extreme that they name: `offset_down`: offset of the scan's window start inside the tile of the device that holds the scan; a window reaches at most into the next tile down, the next tile across and the tile diagonally beyond. `offset_across`: as offset_down, along columns.
All inputs are finite; a program needn't handle non-finite values.
Results may differ from the reference program's by a relative error of at most 0.0001.
Values sent between devices are 32-bit elements; how exact they have to be, the bound alone decides.
No kernel may reach another device: no remote copies, remote signals or barrier semaphores. Data moves between devices by JAX's collectives and lax.ppermute only.
A program may use at most 64 MiB of HBM per device.

```python
import math
import jax
import jax.numpy as jnp
from jax import lax

P_SIZE = 256
MODES = 2
TH = 256
TW = 256
SCAN_DEV = 2
NY = 1024
NX = 2048
SCANS = 64
N_COL = 8


def draw_offset_down(key, part):
    values = jax.random.randint(jax.random.fold_in(key, 11), (SCANS,), 0, TH, dtype=jnp.int32)
    return values.at[0].set(TH - 1).at[1].set(0)


def draw_offset_across(key, part):
    values = jax.random.randint(jax.random.fold_in(key, 23), (SCANS,), 0, TW, dtype=jnp.int32)
    return values.at[1].set(TW - 1).at[0].set(0)


def levels(stream_key, dims, shards, low, high):
    gain, own = 1.0, jax.random.fold_in(stream_key, 6)
    for dim, blocks in shards:
        heights = jnp.exp(jax.random.uniform(jax.random.fold_in(own, dim), (blocks,), jnp.float32, low / len(shards), high / len(shards)))
        gain = gain * jnp.repeat(heights, dims[dim] // blocks).reshape([-1 if axis == dim else 1 for axis in range(len(dims))])
    return gain


def noise(key, dims, width, reach, cuts=(), kind=jnp.bfloat16):
    drawn = jax.random.normal(key, dims, jnp.float32) * width
    if len(cuts) > 0:
        drawn = levels(key, dims, cuts, -0.22, 0.18) * drawn
    return jnp.clip(drawn, min=-reach, max=reach).astype(kind)


def setup_inputs(seed: int = 0) -> dict:
    seeds = jax.random.split(jax.random.key(seed), 6)
    return {
        "transmission": noise(seeds[0], (2, NY, NX), 0.7, 5.0, ((1, 4), (2, 8)), jnp.float32),
        "probe_modes": noise(seeds[1], (MODES, 2, P_SIZE, P_SIZE), 0.7, 5.0, (), jnp.float32),
        "measured": jnp.clip(jnp.exp(math.log(8.0) - 3.6888794 * jax.random.uniform(seeds[2], (SCANS, P_SIZE, P_SIZE), jnp.float32) ** levels(seeds[2], (SCANS, P_SIZE, P_SIZE), ((0, 32),), -0.2, 0.2)), 0.2, 8.0),
        "offset_down": draw_offset_down(jax.random.fold_in(seeds[5], 71), 0),
        "offset_across": draw_offset_across(jax.random.fold_in(seeds[5], 71), 0),
    }


def reference(transmission, probe_modes, measured, offset_down, offset_across):
    padded = jnp.pad(transmission, ((0, 0), (0, P_SIZE), (0, P_SIZE)))
    modes = probe_modes[:, 0] + 1j * probe_modes[:, 1]

    def one_scan(which, carry):
        field, probe_total = carry
        device = which // SCAN_DEV
        top = (device // N_COL * TH + offset_down[which]).astype(jnp.int32)
        start_col = (device % N_COL * TW + offset_across[which]).astype(jnp.int32)
        zero = jnp.int32(0)
        window = lax.dynamic_slice(padded, (zero, top, start_col), (2, P_SIZE, P_SIZE))
        patch = window[0] + 1j * window[1]
        wave = jnp.fft.fft2(modes * patch[None], norm='ortho')
        resid = lax.optimization_barrier(jnp.sum(jnp.real(wave) ** 2 + jnp.imag(wave) ** 2, axis=0)) - measured[which]
        back = jnp.fft.ifft2(resid[None] * wave, norm='ortho')
        object_term = lax.optimization_barrier(jnp.sum(jnp.conj(modes) * back, axis=0))
        probe_term = jnp.conj(patch)[None] * back
        current = lax.dynamic_slice(field, (zero, top, start_col), (2, P_SIZE, P_SIZE))
        update = jnp.stack([jnp.real(object_term), jnp.imag(object_term)])
        field = lax.dynamic_update_slice(field, current + update, (zero, top, start_col))
        probe_total = probe_total + jnp.stack([jnp.real(probe_term), jnp.imag(probe_term)], axis=1)
        return (field, probe_total)
    start = (jnp.zeros_like(padded), jnp.zeros(probe_modes.shape, probe_modes.dtype))
    field, probe_total = lax.fori_loop(0, SCANS, one_scan, start)
    return (field[:, :NY, :NX], probe_total * (1.0 / math.sqrt(SCANS)))
```

```python
import functools
import math

import jax
import jax.numpy as jnp
import numpy as np
from jax import lax
from jax.experimental import pallas as pl
from jax.experimental.pallas import tpu as pltpu
from jax.sharding import PartitionSpec as P

VMEM = pltpu.VMEM
SMEM = pltpu.SMEM


def shifted(block, axis, distance):
    count = lax.axis_size(axis)
    route = [(i - distance, i) for i in range(count) if 0 <= i - distance < count]
    return lax.ppermute(block, axis, route)


def swapped(block, axis, mask):
    return lax.ppermute(block, axis, [(i, i ^ mask) for i in range(lax.axis_size(axis))])


def power_of_two(number):
    return number & (number - 1) == 0


def scatter_sum(values, axis):
    count = lax.axis_size(axis)
    place = lax.axis_index(axis)
    pieces = values.reshape((count, values.shape[0] // count) + values.shape[1:])
    if count > 4 or not power_of_two(count):
        return jnp.sum(lax.all_to_all(pieces, axis, 0, 0), axis=0)
    total = lax.dynamic_index_in_dim(pieces, place, 0, keepdims=False)
    parts = [
        swapped(lax.dynamic_index_in_dim(pieces, place ^ mask, 0, keepdims=False), axis, mask)
        for mask in range(1, count)
    ]
    for part in parts:
        total = total + part
    return total


def gather_slices(piece, axis):
    count = lax.axis_size(axis)
    place = lax.axis_index(axis)
    if count > 4 or not power_of_two(count):
        copies = jnp.broadcast_to(piece[None], (count,) + piece.shape)
        return lax.all_to_all(copies, axis, 0, 0)
    parts = [piece] + [swapped(piece, axis, mask) for mask in range(1, count)]
    stacked = jnp.zeros((count,) + piece.shape, piece.dtype)
    for mask, part in enumerate(parts):
        stacked = lax.dynamic_update_index_in_dim(stacked, part, place ^ mask, 0)
    return stacked


def sum_over_pairs(piece, axis):
    count = lax.axis_size(axis)
    if power_of_two(count):
        mask = 2
        while mask < count:
            piece = piece + swapped(piece, axis, mask)
            mask *= 2
        return piece
    groups = [list(range(parity, count, 2)) for parity in range(2)]
    copies = jnp.broadcast_to(piece[None], (count // 2,) + piece.shape)
    return jnp.sum(lax.all_to_all(copies, axis, 0, 0, axis_index_groups=groups), axis=0)


def split_table(table):
    high = table.astype(jnp.bfloat16)
    low = (table - high.astype(np.float64)).astype(jnp.bfloat16)
    return high, low


def tables(length):
    half = length // 2
    counter = np.arange(half)
    angles = 2.0 * math.pi * (np.outer(counter, counter) % half) / half
    cosines = np.cos(angles) / math.sqrt(length)
    sines = np.sin(angles) / math.sqrt(length)
    forward = np.block([[cosines, -sines], [sines, cosines]])
    backward = np.block([[cosines, sines], [-sines, cosines]])
    result = {}
    for name, table in (("f", forward), ("b", backward)):
        high, low = split_table(table)
        result["right_" + name] = np.concatenate([high, high, low], axis=0)
        high, low = split_table(np.ascontiguousarray(table.T))
        result["left_" + name] = np.concatenate([high, high, low], axis=1)
    turn = 2.0 * math.pi * counter / length
    result["lane"] = np.stack([np.cos(turn), np.sin(turn)]).astype(np.float32)
    across = np.stack([np.cos(turn), np.sin(turn)]).astype(np.float32)
    result["sub"] = np.ascontiguousarray(np.repeat(across[:, :, None], half, axis=2))
    order = np.concatenate([np.arange(0, length, 2), np.arange(1, length, 2)])
    select = np.zeros((length, length), np.float32)
    select[order, np.arange(length)] = 1.0
    result["pick_cols"] = np.concatenate([select] * 3, axis=0).astype(jnp.bfloat16)
    result["pick_rows"] = np.concatenate([select.T] * 3, axis=1).astype(jnp.bfloat16)
    return result


def halves(values):
    high = values.astype(jnp.bfloat16)
    low = (values - high.astype(jnp.float32)).astype(jnp.bfloat16)
    return high, low


def dot(left, right):
    return jnp.dot(left, right, preferred_element_type=jnp.float32)


def thirds(values):
    high = values.astype(jnp.bfloat16)
    rest = values - high.astype(jnp.float32)
    middle = rest.astype(jnp.bfloat16)
    low = (rest - middle.astype(jnp.float32)).astype(jnp.bfloat16)
    return [high, middle, low]


def order_kernel(measured_ref, pick_rows_ref, pick_cols_ref, out_ref):
    scans, length, _ = measured_ref.shape
    half = length // 2
    for which in range(scans):
        rows = dot(pick_rows_ref[...], jnp.concatenate(thirds(measured_ref[which]), axis=0))
        both = dot(jnp.concatenate(thirds(rows), axis=1), pick_cols_ref[...])
        out_ref[which, :, :length] = both[:half]
        out_ref[which, :, length:] = both[half:]


def scan_kernel(
    scalars_ref,
    own_ref,
    right_ref,
    below_ref,
    corner_ref,
    probe_ref,
    measured_ref,
    right_f_ref,
    right_b_ref,
    left_f_ref,
    left_b_ref,
    lane_ref,
    sub_ref,
    own_out,
    right_out,
    below_out,
    corner_out,
    probe_out,
    wave_ref,
):
    scans = measured_ref.shape[0]
    modes, _, length, _ = probe_ref.shape
    half = length // 2
    core = scalars_ref[2 * scans]
    row_of = lax.broadcasted_iota(jnp.int32, (length, length), 0)
    col_of = lax.broadcasted_iota(jnp.int32, (length, length), 1)

    def apply_right(parts, table_ref):
        high, low = halves(parts)
        return dot(jnp.concatenate([high, low, high], axis=1), table_ref[...])

    def apply_left(table_ref, parts):
        high, low = halves(parts)
        return dot(table_ref[...], jnp.concatenate([high, low, high], axis=0))

    def lane_turn():
        return lane_ref[0:1, :], lane_ref[1:2, :]

    for which in range(scans):
        down = scalars_ref[which]
        across = scalars_ref[scans + which]
        later_row = row_of < down
        later_col = col_of < across
        up = lax.rem(length - down, length)
        back_across = lax.rem(length - across, length)
        patch = []
        for part in range(2):
            merged = jnp.where(
                later_row,
                jnp.where(later_col, corner_ref[part], below_ref[part]),
                jnp.where(later_col, right_ref[part], own_ref[part]),
            )
            patch.append(pltpu.roll(pltpu.roll(merged, up, 0), back_across, 1))
        patch_r, patch_i = patch

        intensity = None
        for mode in range(modes):
            probe_r, probe_i = probe_ref[mode, 0], probe_ref[mode, 1]
            exit_r = probe_r * patch_r - probe_i * patch_i
            exit_i = probe_r * patch_i + probe_i * patch_r
            cos, sin = lane_turn()
            first_r, last_r = exit_r[:, :half], exit_r[:, half:]
            first_i, last_i = exit_i[:, :half], exit_i[:, half:]
            gap_r, gap_i = first_r - last_r, first_i - last_i
            even = jnp.concatenate([first_r + last_r, first_i + last_i], axis=1)
            odd = jnp.concatenate(
                [gap_r * cos + gap_i * sin, gap_i * cos - gap_r * sin], axis=1
            )
            even = apply_right(even, right_f_ref)
            odd = apply_right(odd, right_f_ref)
            cos, sin = sub_ref[0], sub_ref[1]
            sums, turned = [[], []], [[], []]
            for block in (even, odd):
                top_r, low_r = block[:half, :half], block[half:, :half]
                top_i, low_i = block[:half, half:], block[half:, half:]
                gap_r, gap_i = top_r - low_r, top_i - low_i
                sums[0].append(top_r + low_r)
                sums[1].append(top_i + low_i)
                turned[0].append(gap_r * cos + gap_i * sin)
                turned[1].append(gap_i * cos - gap_r * sin)
            stacked = jnp.concatenate(
                [jnp.concatenate(sums[part] + turned[part], axis=1) for part in range(2)], axis=0
            )
            wave = apply_left(left_f_ref, stacked)
            wave_ref[mode] = wave
            wave_r, wave_i = wave[:half], wave[half:]
            square = wave_r * wave_r + wave_i * wave_i
            intensity = square if intensity is None else intensity + square
        resid = intensity - measured_ref[which]

        object_r = object_i = None
        for mode in range(modes):
            wave = wave_ref[mode]
            weighted = jnp.concatenate([resid * wave[:half], resid * wave[half:]], axis=0)
            rows = apply_left(left_b_ref, weighted)
            cos, sin = sub_ref[0], sub_ref[1]
            cos = jnp.concatenate([cos, cos], axis=1)
            sin = jnp.concatenate([sin, sin], axis=1)
            even_r, odd_r = rows[:half, :length], rows[:half, length:]
            even_i, odd_i = rows[half:, :length], rows[half:, length:]
            turn_r = odd_r * cos - odd_i * sin
            turn_i = odd_i * cos + odd_r * sin
            real = jnp.concatenate([even_r + turn_r, even_r - turn_r], axis=0)
            imag = jnp.concatenate([even_i + turn_i, even_i - turn_i], axis=0)
            even = jnp.concatenate([real[:, :half], imag[:, :half]], axis=1)
            odd = jnp.concatenate([real[:, half:], imag[:, half:]], axis=1)
            even = apply_right(even, right_b_ref)
            odd = apply_right(odd, right_b_ref)
            cos, sin = lane_turn()
            turn_r = odd[:, :half] * cos - odd[:, half:] * sin
            turn_i = odd[:, half:] * cos + odd[:, :half] * sin
            back_r = jnp.concatenate([even[:, :half] + turn_r, even[:, :half] - turn_r], axis=1)
            back_i = jnp.concatenate([even[:, half:] + turn_i, even[:, half:] - turn_i], axis=1)
            slot = mode ^ core if modes == 2 else mode
            term_r = patch_r * back_r + patch_i * back_i
            term_i = patch_r * back_i - patch_i * back_r
            if which == 0:
                probe_out[slot, 0] = term_r
                probe_out[slot, 1] = term_i
            else:
                probe_out[slot, 0] = probe_out[slot, 0] + term_r
                probe_out[slot, 1] = probe_out[slot, 1] + term_i
            probe_r, probe_i = probe_ref[mode, 0], probe_ref[mode, 1]
            term_r = probe_r * back_r + probe_i * back_i
            term_i = probe_r * back_i - probe_i * back_r
            object_r = term_r if object_r is None else object_r + term_r
            object_i = term_i if object_i is None else object_i + term_i

        for part, values in ((0, object_r), (1, object_i)):
            placed = pltpu.roll(pltpu.roll(values, down, 0), across, 1)
            upper = jnp.where(later_row, 0.0, placed)
            lower = jnp.where(later_row, placed, 0.0)
            pieces = (
                (own_out, jnp.where(later_col, 0.0, upper)),
                (right_out, jnp.where(later_col, upper, 0.0)),
                (below_out, jnp.where(later_col, 0.0, lower)),
                (corner_out, jnp.where(later_col, lower, 0.0)),
            )
            for out, piece in pieces:
                if which == 0:
                    out[part] = piece
                else:
                    out[part] = out[part] + piece


def whole():
    return pl.BlockSpec(memory_space=VMEM)


def order_measured(measured, pick_rows, pick_cols):
    scans, length, _ = measured.shape
    return pl.pallas_call(
        order_kernel,
        out_shape=jax.ShapeDtypeStruct((scans, length // 2, 2 * length), jnp.float32),
        in_specs=[whole()] * 3,
        out_specs=whole(),
        name="order_measured",
    )(measured, pick_rows, pick_cols)


def process_scans(scalars, tiles, probe_modes, measured, consts):
    tile = jax.ShapeDtypeStruct(tiles[0].shape, jnp.float32)
    modes, _, length, _ = probe_modes.shape
    return pl.pallas_call(
        scan_kernel,
        out_shape=[tile] * 4 + [jax.ShapeDtypeStruct(probe_modes.shape, jnp.float32)],
        in_specs=[pl.BlockSpec(memory_space=SMEM)] + [whole()] * 12,
        out_specs=[whole()] * 5,
        scratch_shapes=[pltpu.VMEM((modes, length, 2 * length), jnp.float32)],
        compiler_params=pltpu.CompilerParams(vmem_limit_bytes=56 * 1024 * 1024),
        name="process_scans",
    )(scalars, *tiles, probe_modes, measured, *consts)


def on_device(transmission, probe_modes, measured, offset_down, offset_across):
    length = probe_modes.shape[-1]
    scan_count = measured.shape[0]
    core = lax.axis_index("col") % 2
    table = tables(length)
    below = shifted(transmission, "row", -1)
    right = shifted(transmission, "col", -1)
    corner = shifted(below, "col", -1)
    ordered = order_measured(measured, table["pick_rows"], table["pick_cols"])
    scalars = jnp.concatenate([offset_down, offset_across, core.astype(jnp.int32)[None]])
    consts = [table[name] for name in ("right_f", "right_b", "left_f", "left_b", "lane", "sub")]
    own, to_right, to_below, to_corner, probe_terms = process_scans(
        scalars, (transmission, right, below, corner), probe_modes, ordered, consts
    )

    mine = probe_terms[0] + swapped(probe_terms[1], "col", 1)
    piece = scatter_sum(mine.reshape((-1, length)), "row")
    piece = sum_over_pairs(piece, "col")
    scans_total = scan_count * lax.axis_size("row") * lax.axis_size("col")
    piece = piece * (1.0 / math.sqrt(scans_total))
    mine = gather_slices(piece, "row").reshape(mine.shape)
    other = swapped(mine, "col", 1)
    first = core == 0
    probe_gradient = jnp.stack([jnp.where(first, mine, other), jnp.where(first, other, mine)])

    to_below = to_below + shifted(to_corner, "col", 1)
    own = own + shifted(to_right, "col", 1) + shifted(to_below, "row", 1)
    return own, probe_gradient


def solution(mesh):
    in_specs = (
        P(None, "row", "col"),
        P(),
        P(("row", "col"), None, None),
        P(("row", "col")),
        P(("row", "col")),
    )
    out_specs = (P(None, "row", "col"), P())
    return jax.shard_map(
        on_device, mesh=mesh, in_specs=in_specs, out_specs=out_specs, check_vma=False
    )
```

```python
import math

import jax
import jax.numpy as jnp
import numpy as np
from jax import lax
from jax.experimental import pallas as pl
from jax.experimental.pallas import tpu as pltpu
from jax.sharding import PartitionSpec as P


VMEM = pltpu.VMEM
SMEM = pltpu.SMEM
PREPARE_VMEM = 8 * 1024 * 1024
PROCESS_VMEM = 20 * 1024 * 1024


def shifted(block, axis, distance):
    count = lax.axis_size(axis)
    route = [(i - distance, i) for i in range(count) if 0 <= i - distance < count]
    return lax.ppermute(block, axis, route)


def swapped(block, axis, mask):
    return lax.ppermute(block, axis, [(i, i ^ mask) for i in range(lax.axis_size(axis))])


def power_of_two(number):
    return number & (number - 1) == 0


def chip_groups(parts):
    rows, cols = lax.axis_size("row"), lax.axis_size("col")
    return [
        [row * cols + first + core + 2 * part for row in range(rows) for part in range(parts)]
        for first in range(0, cols, 2 * parts)
        for core in range(2)
    ]


def scatter_sum(values, groups):
    count = len(groups[0])
    pieces = values.reshape((count, values.shape[0] // count) + values.shape[1:])
    return jnp.sum(
        lax.all_to_all(pieces, ("row", "col"), 0, 0, axis_index_groups=groups), axis=0
    )


def gather_slices(piece, groups):
    copies = jnp.broadcast_to(piece[None], (len(groups[0]),) + piece.shape)
    slices = lax.all_to_all(copies, ("row", "col"), 0, 0, axis_index_groups=groups)
    return slices.reshape((-1,) + piece.shape[1:])


def sum_over_groups(piece, stride):
    count = lax.axis_size("col")
    if power_of_two(count // stride):
        mask = stride
        while mask < count:
            piece = piece + swapped(piece, "col", mask)
            mask *= 2
        return piece
    groups = [list(range(first, count, stride)) for first in range(stride)]
    copies = jnp.broadcast_to(piece[None], (count // stride,) + piece.shape)
    return jnp.sum(lax.all_to_all(copies, "col", 0, 0, axis_index_groups=groups), axis=0)


def split_table(table):
    high = table.astype(jnp.bfloat16)
    low = (table - high.astype(np.float64)).astype(jnp.bfloat16)
    return high, low


def tables(length):
    half = length // 2
    counter = np.arange(half)
    angles = 2.0 * math.pi * (np.outer(counter, counter) % half) / half
    cosines = np.cos(angles) / math.sqrt(length)
    sines = np.sin(angles) / math.sqrt(length)
    forward = np.block([[cosines, -sines], [sines, cosines]])
    backward = np.block([[cosines, sines], [-sines, cosines]])
    result = {}
    for name, table in (("f", forward), ("b", backward)):
        high, low = split_table(table)
        result["right_" + name] = np.concatenate([high, high, low], axis=0)
        high, low = split_table(np.ascontiguousarray(table.T))
        result["left_" + name] = np.concatenate([high, high, low], axis=1)
    turn = 2.0 * math.pi * counter / length
    result["lane"] = np.stack([np.cos(turn), np.sin(turn)]).astype(np.float32)
    across = np.stack([np.cos(turn), np.sin(turn)]).astype(np.float32)
    result["sub"] = np.ascontiguousarray(np.repeat(across[:, :, None], half, axis=2))
    order = np.concatenate([np.arange(0, length, 2), np.arange(1, length, 2)])
    select = np.zeros((length, length), np.float32)
    select[order, np.arange(length)] = 1.0
    result["pick_cols"] = np.concatenate([select] * 3, axis=0).astype(jnp.bfloat16)
    result["pick_rows"] = np.concatenate([select.T] * 3, axis=1).astype(jnp.bfloat16)
    return result


def halves(values):
    high = values.astype(jnp.bfloat16)
    low = (values - high.astype(jnp.float32)).astype(jnp.bfloat16)
    return high, low


def dot(left, right):
    return jnp.dot(left, right, preferred_element_type=jnp.float32)


def thirds(values):
    high = values.astype(jnp.bfloat16)
    rest = values - high.astype(jnp.float32)
    middle = rest.astype(jnp.bfloat16)
    low = (rest - middle.astype(jnp.float32)).astype(jnp.bfloat16)
    return [high, middle, low]


def prepare_kernel(measured_ref, pick_rows_ref, pick_cols_ref, *refs):
    out_ref = refs[-1]
    for source, target in zip(refs[: len(refs) // 2], refs[len(refs) // 2 :]):
        target[...] = source[...]
    scans, length, _ = measured_ref.shape
    half = length // 2
    for which in range(scans):
        rows = dot(pick_rows_ref[...], jnp.concatenate(thirds(measured_ref[which]), axis=0))
        both = dot(jnp.concatenate(thirds(rows), axis=1), pick_cols_ref[...])
        out_ref[which, :, :length] = both[:half]
        out_ref[which, :, length:] = both[half:]


def scan_kernel(
    down_ref,
    across_ref,
    own_ref,
    right_ref,
    below_ref,
    corner_ref,
    relayed_ref,
    probe_ref,
    measured_ref,
    right_f_ref,
    left_f_ref,
    left_b_ref,
    right_b_ref,
    lane_ref,
    sub_ref,
    own_out,
    right_out,
    below_out,
    corner_out,
    keep_out,
    send_out,
    wave_ref,
):
    scans = measured_ref.shape[0]
    modes, _, length, _ = probe_ref.shape
    half = length // 2
    core = lax.rem(lax.axis_index("col"), 2)
    row_of = lax.broadcasted_iota(jnp.int32, (length, length), 0)
    col_of = lax.broadcasted_iota(jnp.int32, (length, length), 1)

    def apply_right(parts, table_ref):
        high, low = halves(parts)
        return dot(jnp.concatenate([high, low, high], axis=1), table_ref[...])

    def apply_left(table_ref, parts):
        high, low = halves(parts)
        return dot(table_ref[...], jnp.concatenate([high, low, high], axis=0))

    def lane_turn():
        return lane_ref[0:1, :], lane_ref[1:2, :]

    for which in range(scans):
        down = down_ref[which]
        across = across_ref[which]
        later_row = row_of < down
        later_col = col_of < across
        up = lax.rem(length - down, length)
        back_across = lax.rem(length - across, length)
        patch = []
        for part in range(2):
            merged = jnp.where(
                later_row,
                jnp.where(later_col, corner_ref[part] + relayed_ref[part], below_ref[part]),
                jnp.where(later_col, right_ref[part], own_ref[part]),
            )
            patch.append(pltpu.roll(pltpu.roll(merged, up, 0), back_across, 1))
        patch_r, patch_i = patch

        intensity = None
        for step in range(modes):
            mode = step ^ core
            probe_r, probe_i = probe_ref[mode, 0], probe_ref[mode, 1]
            exit_r = probe_r * patch_r - probe_i * patch_i
            exit_i = probe_r * patch_i + probe_i * patch_r
            cos, sin = lane_turn()
            first_r, last_r = exit_r[:, :half], exit_r[:, half:]
            first_i, last_i = exit_i[:, :half], exit_i[:, half:]
            gap_r, gap_i = first_r - last_r, first_i - last_i
            even = jnp.concatenate([first_r + last_r, first_i + last_i], axis=1)
            odd = jnp.concatenate(
                [gap_r * cos + gap_i * sin, gap_i * cos - gap_r * sin], axis=1
            )
            even = apply_right(even, right_f_ref)
            odd = apply_right(odd, right_f_ref)
            cos, sin = sub_ref[0], sub_ref[1]
            sums, turned = [[], []], [[], []]
            for block in (even, odd):
                top_r, low_r = block[:half, :half], block[half:, :half]
                top_i, low_i = block[:half, half:], block[half:, half:]
                gap_r, gap_i = top_r - low_r, top_i - low_i
                sums[0].append(top_r + low_r)
                sums[1].append(top_i + low_i)
                turned[0].append(gap_r * cos + gap_i * sin)
                turned[1].append(gap_i * cos - gap_r * sin)
            stacked = jnp.concatenate(
                [jnp.concatenate(sums[part] + turned[part], axis=1) for part in range(2)], axis=0
            )
            wave = apply_left(left_f_ref, stacked)
            wave_ref[step] = wave
            wave_r, wave_i = wave[:half], wave[half:]
            square = wave_r * wave_r + wave_i * wave_i
            intensity = square if intensity is None else intensity + square
        resid = intensity - measured_ref[which]

        object_r = object_i = None
        for step in range(modes):
            mode = step ^ core
            wave = wave_ref[step]
            weighted = jnp.concatenate([resid * wave[:half], resid * wave[half:]], axis=0)
            rows = apply_left(left_b_ref, weighted)
            cos, sin = sub_ref[0], sub_ref[1]
            cos = jnp.concatenate([cos, cos], axis=1)
            sin = jnp.concatenate([sin, sin], axis=1)
            even_r, odd_r = rows[:half, :length], rows[:half, length:]
            even_i, odd_i = rows[half:, :length], rows[half:, length:]
            turn_r = odd_r * cos - odd_i * sin
            turn_i = odd_i * cos + odd_r * sin
            real = jnp.concatenate([even_r + turn_r, even_r - turn_r], axis=0)
            imag = jnp.concatenate([even_i + turn_i, even_i - turn_i], axis=0)
            even = jnp.concatenate([real[:, :half], imag[:, :half]], axis=1)
            odd = jnp.concatenate([real[:, half:], imag[:, half:]], axis=1)
            even = apply_right(even, right_b_ref)
            odd = apply_right(odd, right_b_ref)
            cos, sin = lane_turn()
            turn_r = odd[:, :half] * cos - odd[:, half:] * sin
            turn_i = odd[:, half:] * cos + odd[:, :half] * sin
            back_r = jnp.concatenate([even[:, :half] + turn_r, even[:, :half] - turn_r], axis=1)
            back_i = jnp.concatenate([even[:, half:] + turn_i, even[:, half:] - turn_i], axis=1)
            probe_out = (keep_out, send_out)[step]
            term_r = patch_r * back_r + patch_i * back_i
            term_i = patch_r * back_i - patch_i * back_r
            if which == 0:
                probe_out[0] = term_r
                probe_out[1] = term_i
            else:
                probe_out[0] = probe_out[0] + term_r
                probe_out[1] = probe_out[1] + term_i
            probe_r, probe_i = probe_ref[mode, 0], probe_ref[mode, 1]
            term_r = probe_r * back_r + probe_i * back_i
            term_i = probe_r * back_i - probe_i * back_r
            object_r = term_r if object_r is None else object_r + term_r
            object_i = term_i if object_i is None else object_i + term_i

        for part, values in ((0, object_r), (1, object_i)):
            placed = pltpu.roll(pltpu.roll(values, down, 0), across, 1)
            upper = jnp.where(later_row, 0.0, placed)
            lower = jnp.where(later_row, placed, 0.0)
            pieces = (
                (own_out, jnp.where(later_col, 0.0, upper)),
                (right_out, jnp.where(later_col, upper, 0.0)),
                (below_out, jnp.where(later_col, 0.0, lower)),
                (corner_out, jnp.where(later_col, lower, 0.0)),
            )
            for out, piece in pieces:
                if which == 0:
                    out[part] = piece
                else:
                    out[part] = out[part] + piece


def in_vmem(*arrays):
    return [pltpu.with_memory_space_constraint(array, VMEM) for array in arrays]


def whole():
    return pl.BlockSpec(memory_space=VMEM)


def prepare(measured, picks, consts):
    scans, length, _ = measured.shape
    shapes = [VMEM(const.shape, const.dtype) for const in consts]
    return pl.pallas_call(
        prepare_kernel,
        out_shape=shapes + [VMEM((scans, length // 2, 2 * length), jnp.float32)],
        in_specs=[whole()] * (3 + len(consts)),
        out_specs=[whole()] * (1 + len(consts)),
        compiler_params=pltpu.CompilerParams(vmem_limit_bytes=PREPARE_VMEM),
        name="prepare",
    )(measured, *picks, *consts)


def process_scans(offsets, tiles, probe_modes, measured, consts):
    modes, _, length, _ = probe_modes.shape
    operands = in_vmem(*tiles, probe_modes, measured, *consts)
    results = [tiles[0].shape] * 4 + [probe_modes.shape[1:]] * 2
    return pl.pallas_call(
        scan_kernel,
        out_shape=[VMEM(shape, jnp.float32) for shape in results],
        in_specs=[pl.BlockSpec(memory_space=SMEM)] * 2 + [whole()] * len(operands),
        out_specs=[whole()] * len(results),
        scratch_shapes=[VMEM((modes, length, 2 * length), jnp.float32)],
        compiler_params=pltpu.CompilerParams(vmem_limit_bytes=PROCESS_VMEM),
        name="process_scans",
    )(*offsets, *operands)


def on_device(transmission, probe_modes, measured, offset_down, offset_across):
    length = probe_modes.shape[-1]
    scan_count = measured.shape[0]
    rows, cols = lax.axis_size("row"), lax.axis_size("col")
    core = lax.rem(lax.axis_index("col"), 2)
    table = tables(length)

    below = shifted(transmission, "row", -1)
    direct = [
        ((row + 1) * cols + col + 1, row * cols + col)
        for row in range(rows - 1)
        for col in range(1, cols - 1, 2)
    ]
    corner = lax.ppermute(transmission, ("row", "col"), direct)
    right = shifted(transmission, "col", -1)
    consts = [table[name] for name in ("right_f", "left_f", "left_b", "right_b", "lane", "sub")]
    picks = [table["pick_rows"], table["pick_cols"]]
    *consts, ordered = prepare(measured, picks, consts)
    relayed = lax.ppermute(below, "col", [(col + 1, col) for col in range(0, cols - 1, 2)])

    offsets = (offset_down, offset_across)
    own, to_right, to_below, to_corner, keep, send = process_scans(
        offsets, (transmission, right, below, corner, relayed), probe_modes, ordered, consts
    )

    keep = keep + swapped(send, "col", 1)
    parts = 2 if cols % 4 == 0 else 1
    groups = chip_groups(parts)
    piece = scatter_sum(keep.reshape((-1, length)), groups)
    piece = sum_over_groups(piece, 2 * parts)
    scans_total = scan_count * rows * cols
    mine = gather_slices(piece * (1.0 / math.sqrt(scans_total)), groups).reshape(keep.shape)
    other = swapped(mine, "col", 1)
    probe_gradient = jnp.zeros(probe_modes.shape, jnp.float32)
    probe_gradient = lax.dynamic_update_index_in_dim(probe_gradient, mine, core, 0)
    probe_gradient = lax.dynamic_update_index_in_dim(probe_gradient, other, 1 - core, 0)

    to_below = to_below + shifted(to_corner, "col", 1)
    own = lax.optimization_barrier(own + shifted(to_right, "col", 1))
    own = own + shifted(to_below, "row", 1)
    return own, probe_gradient


def solution(mesh):
    in_specs = (
        P(None, "row", "col"),
        P(),
        P(("row", "col"), None, None),
        P(("row", "col")),
        P(("row", "col")),
    )
    out_specs = (P(None, "row", "col"), P())
    return jax.shard_map(
        on_device, mesh=mesh, in_specs=in_specs, out_specs=out_specs, check_vma=False
    )
```

```python
import functools
import math

import jax
import jax.numpy as jnp
import numpy as np
from jax import lax
from jax.experimental import pallas as pl
from jax.experimental.pallas import tpu as pltpu
from jax.sharding import PartitionSpec as P


VMEM = pltpu.VMEM
SMEM = pltpu.SMEM
PREPARE_VMEM = 8 * 1024 * 1024
PROCESS_VMEM = 20 * 1024 * 1024


def shifted(block, axis, distance):
    count = lax.axis_size(axis)
    route = [(i - distance, i) for i in range(count) if 0 <= i - distance < count]
    return lax.ppermute(block, axis, route)


def swapped(block, axis, mask):
    return lax.ppermute(block, axis, [(i, i ^ mask) for i in range(lax.axis_size(axis))])


def power_of_two(number):
    return number & (number - 1) == 0


def chip_groups(parts):
    rows, cols = lax.axis_size("row"), lax.axis_size("col")
    return [
        [row * cols + first + core + 2 * part for row in range(rows) for part in range(parts)]
        for first in range(0, cols, 2 * parts)
        for core in range(2)
    ]


def scatter_sum(values, groups):
    count = len(groups[0])
    pieces = values.reshape((count, values.shape[0] // count) + values.shape[1:])
    return jnp.sum(
        lax.all_to_all(pieces, ("row", "col"), 0, 0, axis_index_groups=groups), axis=0
    )


def gather_slices(piece, groups):
    copies = jnp.broadcast_to(piece[None], (len(groups[0]),) + piece.shape)
    slices = lax.all_to_all(copies, ("row", "col"), 0, 0, axis_index_groups=groups)
    return slices.reshape((-1,) + piece.shape[1:])


def sum_over_groups(piece, stride):
    count = lax.axis_size("col")
    if power_of_two(count // stride):
        mask = stride
        while mask < count:
            piece = piece + swapped(piece, "col", mask)
            mask *= 2
        return piece
    groups = [list(range(first, count, stride)) for first in range(stride)]
    copies = jnp.broadcast_to(piece[None], (count // stride,) + piece.shape)
    return jnp.sum(lax.all_to_all(copies, "col", 0, 0, axis_index_groups=groups), axis=0)


def split_table(table):
    high = table.astype(jnp.bfloat16)
    low = (table - high.astype(np.float64)).astype(jnp.bfloat16)
    return high, low


def tables(length):
    half = length // 2
    counter = np.arange(half)
    angles = 2.0 * math.pi * (np.outer(counter, counter) % half) / half
    cosines = np.cos(angles) / math.sqrt(length)
    sines = np.sin(angles) / math.sqrt(length)
    forward = np.block([[cosines, -sines], [sines, cosines]])
    backward = np.block([[cosines, sines], [-sines, cosines]])
    result = {}
    for name, table in (("f", forward), ("b", backward)):
        high, low = split_table(table)
        result["right_" + name] = np.concatenate([high, high, low], axis=0)
        high, low = split_table(np.ascontiguousarray(table.T))
        result["left_" + name] = np.concatenate([high, high, low], axis=1)
    turn = 2.0 * math.pi * counter / length
    result["lane"] = np.stack([np.cos(turn), np.sin(turn)]).astype(np.float32)
    across = np.stack([np.cos(turn), np.sin(turn)]).astype(np.float32)
    result["sub"] = np.ascontiguousarray(np.repeat(across[:, :, None], half, axis=2))
    order = np.concatenate([np.arange(0, length, 2), np.arange(1, length, 2)])
    select = np.zeros((length, length), np.float32)
    select[order, np.arange(length)] = 1.0
    result["pick_cols"] = np.concatenate([select] * 3, axis=0).astype(jnp.bfloat16)
    result["pick_rows"] = np.concatenate([select.T] * 3, axis=1).astype(jnp.bfloat16)
    return result


def halves(values):
    high = values.astype(jnp.bfloat16)
    low = (values - high.astype(jnp.float32)).astype(jnp.bfloat16)
    return high, low


def dot(left, right):
    return jnp.dot(left, right, preferred_element_type=jnp.float32)


def thirds(values):
    high = values.astype(jnp.bfloat16)
    rest = values - high.astype(jnp.float32)
    middle = rest.astype(jnp.bfloat16)
    low = (rest - middle.astype(jnp.float32)).astype(jnp.bfloat16)
    return [high, middle, low]


def prepare_kernel(measured_ref, pick_rows_ref, pick_cols_ref, *refs):
    out_ref = refs[-1]
    for source, target in zip(refs[: len(refs) // 2], refs[len(refs) // 2 :]):
        target[...] = source[...]
    scans, length, _ = measured_ref.shape
    half = length // 2
    for which in range(scans):
        rows = dot(pick_rows_ref[...], jnp.concatenate(thirds(measured_ref[which]), axis=0))
        both = dot(jnp.concatenate(thirds(rows), axis=1), pick_cols_ref[...])
        out_ref[which, :, :length] = both[:half]
        out_ref[which, :, length:] = both[half:]


def scan_kernel(
    down_ref,
    across_ref,
    own_ref,
    right_ref,
    below_first_ref,
    below_last_ref,
    corner_first_ref,
    corner_last_ref,
    relayed_ref,
    probe_ref,
    measured_ref,
    right_f_ref,
    left_f_ref,
    left_b_ref,
    right_b_ref,
    lane_ref,
    sub_ref,
    own_out,
    right_out,
    below_out,
    corner_out,
    keep_out,
    send_out,
    wave_ref,
):
    scans = measured_ref.shape[0]
    modes, _, length, _ = probe_ref.shape
    half = length // 2
    core = lax.rem(lax.axis_index("col"), 2)
    row_of = lax.broadcasted_iota(jnp.int32, (length, length), 0)
    col_of = lax.broadcasted_iota(jnp.int32, (length, length), 1)

    def apply_right(parts, table_ref):
        high, low = halves(parts)
        return dot(jnp.concatenate([high, low, high], axis=1), table_ref[...])

    def apply_left(table_ref, parts):
        high, low = halves(parts)
        return dot(table_ref[...], jnp.concatenate([high, low, high], axis=0))

    def lane_turn():
        return lane_ref[0:1, :], lane_ref[1:2, :]

    for which in range(scans):
        down = down_ref[which]
        across = across_ref[which]
        later_row = row_of < down
        later_col = col_of < across
        up = lax.rem(length - down, length)
        back_across = lax.rem(length - across, length)
        patch = []
        for part in range(2):
            below = jnp.concatenate([below_first_ref[part], below_last_ref[part]], axis=0)
            corner_last = corner_last_ref[part] + relayed_ref[part]
            corner = jnp.concatenate([corner_first_ref[part], corner_last], axis=0)
            merged = jnp.where(
                later_row,
                jnp.where(later_col, corner, below),
                jnp.where(later_col, right_ref[part], own_ref[part]),
            )
            patch.append(pltpu.roll(pltpu.roll(merged, up, 0), back_across, 1))
        patch_r, patch_i = patch

        intensity = None
        for step in range(modes):
            mode = step ^ core
            probe_r, probe_i = probe_ref[mode, 0], probe_ref[mode, 1]
            exit_r = probe_r * patch_r - probe_i * patch_i
            exit_i = probe_r * patch_i + probe_i * patch_r
            cos, sin = lane_turn()
            first_r, last_r = exit_r[:, :half], exit_r[:, half:]
            first_i, last_i = exit_i[:, :half], exit_i[:, half:]
            gap_r, gap_i = first_r - last_r, first_i - last_i
            even = jnp.concatenate([first_r + last_r, first_i + last_i], axis=1)
            odd = jnp.concatenate(
                [gap_r * cos + gap_i * sin, gap_i * cos - gap_r * sin], axis=1
            )
            even = apply_right(even, right_f_ref)
            odd = apply_right(odd, right_f_ref)
            cos, sin = sub_ref[0], sub_ref[1]
            sums, turned = [[], []], [[], []]
            for block in (even, odd):
                top_r, low_r = block[:half, :half], block[half:, :half]
                top_i, low_i = block[:half, half:], block[half:, half:]
                gap_r, gap_i = top_r - low_r, top_i - low_i
                sums[0].append(top_r + low_r)
                sums[1].append(top_i + low_i)
                turned[0].append(gap_r * cos + gap_i * sin)
                turned[1].append(gap_i * cos - gap_r * sin)
            stacked = jnp.concatenate(
                [jnp.concatenate(sums[part] + turned[part], axis=1) for part in range(2)], axis=0
            )
            wave = apply_left(left_f_ref, stacked)
            wave_ref[step] = wave
            wave_r, wave_i = wave[:half], wave[half:]
            square = wave_r * wave_r + wave_i * wave_i
            intensity = square if intensity is None else intensity + square
        resid = intensity - measured_ref[which]

        object_r = object_i = None
        for step in range(modes):
            mode = step ^ core
            wave = wave_ref[step]
            weighted = jnp.concatenate([resid * wave[:half], resid * wave[half:]], axis=0)
            rows = apply_left(left_b_ref, weighted)
            cos, sin = sub_ref[0], sub_ref[1]
            cos = jnp.concatenate([cos, cos], axis=1)
            sin = jnp.concatenate([sin, sin], axis=1)
            even_r, odd_r = rows[:half, :length], rows[:half, length:]
            even_i, odd_i = rows[half:, :length], rows[half:, length:]
            turn_r = odd_r * cos - odd_i * sin
            turn_i = odd_i * cos + odd_r * sin
            real = jnp.concatenate([even_r + turn_r, even_r - turn_r], axis=0)
            imag = jnp.concatenate([even_i + turn_i, even_i - turn_i], axis=0)
            even = jnp.concatenate([real[:, :half], imag[:, :half]], axis=1)
            odd = jnp.concatenate([real[:, half:], imag[:, half:]], axis=1)
            even = apply_right(even, right_b_ref)
            odd = apply_right(odd, right_b_ref)
            cos, sin = lane_turn()
            turn_r = odd[:, :half] * cos - odd[:, half:] * sin
            turn_i = odd[:, half:] * cos + odd[:, :half] * sin
            back_r = jnp.concatenate([even[:, :half] + turn_r, even[:, :half] - turn_r], axis=1)
            back_i = jnp.concatenate([even[:, half:] + turn_i, even[:, half:] - turn_i], axis=1)
            probe_out = (keep_out, send_out)[step]
            term_r = patch_r * back_r + patch_i * back_i
            term_i = patch_r * back_i - patch_i * back_r
            if which == 0:
                probe_out[0] = term_r
                probe_out[1] = term_i
            else:
                probe_out[0] = probe_out[0] + term_r
                probe_out[1] = probe_out[1] + term_i
            probe_r, probe_i = probe_ref[mode, 0], probe_ref[mode, 1]
            term_r = probe_r * back_r + probe_i * back_i
            term_i = probe_r * back_i - probe_i * back_r
            object_r = term_r if object_r is None else object_r + term_r
            object_i = term_i if object_i is None else object_i + term_i

        for part, values in ((0, object_r), (1, object_i)):
            placed = pltpu.roll(pltpu.roll(values, down, 0), across, 1)
            upper = jnp.where(later_row, 0.0, placed)
            lower = jnp.where(later_row, placed, 0.0)
            pieces = (
                (own_out, jnp.where(later_col, 0.0, upper)),
                (right_out, jnp.where(later_col, upper, 0.0)),
                (below_out, jnp.where(later_col, 0.0, lower)),
                (corner_out, jnp.where(later_col, lower, 0.0)),
            )
            for out, piece in pieces:
                if which == 0:
                    out[part] = piece
                else:
                    out[part] = out[part] + piece


def in_space(space, *arrays):
    return [pltpu.with_memory_space_constraint(array, space) for array in arrays]


def whole():
    return pl.BlockSpec(memory_space=VMEM)


def prepare(measured, picks, consts):
    scans, length, _ = measured.shape
    shapes = [VMEM(const.shape, const.dtype) for const in consts]
    return pl.pallas_call(
        prepare_kernel,
        out_shape=shapes + [VMEM((scans, length // 2, 2 * length), jnp.float32)],
        in_specs=[whole()] * (3 + len(consts)),
        out_specs=[whole()] * (1 + len(consts)),
        compiler_params=pltpu.CompilerParams(vmem_limit_bytes=PREPARE_VMEM),
        name="prepare",
    )(*in_space(pltpu.HBM, measured, *picks, *consts))


def process_scans(offsets, tiles, probe_modes, measured, consts):
    modes, _, length, _ = probe_modes.shape
    operands = in_space(VMEM, *tiles, probe_modes, measured, *consts)
    results = [tiles[0].shape] * 4 + [probe_modes.shape[1:]] * 2
    return pl.pallas_call(
        scan_kernel,
        out_shape=[VMEM(shape, jnp.float32) for shape in results],
        in_specs=[pl.BlockSpec(memory_space=SMEM)] * 2 + [whole()] * len(operands),
        out_specs=[whole()] * len(results),
        scratch_shapes=[VMEM((modes, length, 2 * length), jnp.float32)],
        compiler_params=pltpu.CompilerParams(vmem_limit_bytes=PROCESS_VMEM),
        name="process_scans",
    )(*offsets, *operands)


def place_kernel(step, values_ref, *refs):
    out_ref, sem = refs[-2], refs[-1]
    mode = lax.rem(lax.axis_index("col"), 2) ^ step
    copy = pltpu.make_async_copy(values_ref, out_ref.at[mode], sem)
    copy.start()
    copy.wait()


def place_mode(values, modes, step, into=None):
    before = () if into is None else (into,)
    return pl.pallas_call(
        functools.partial(place_kernel, step),
        out_shape=jax.ShapeDtypeStruct((modes,) + values.shape, values.dtype),
        in_specs=[whole()] + [pl.BlockSpec(memory_space=pl.ANY)] * len(before),
        out_specs=pl.BlockSpec(memory_space=pl.ANY),
        scratch_shapes=[pltpu.SemaphoreType.DMA],
        input_output_aliases={1: 0} if before else {},
        compiler_params=pltpu.CompilerParams(vmem_limit_bytes=PREPARE_VMEM),
        name="place_mode",
    )(*in_space(VMEM, values), *before)


def add_kernel(*refs):
    total = refs[0][...]
    for ref in refs[1:-1]:
        total = total + ref[...]
    refs[-1][...] = total


def add_tiles(*tiles, out):
    return pl.pallas_call(
        add_kernel,
        out_shape=out,
        in_specs=[whole()] * len(tiles),
        out_specs=whole(),
        compiler_params=pltpu.CompilerParams(vmem_limit_bytes=PREPARE_VMEM),
        name="add_tiles",
    )(*in_space(VMEM, *tiles))


def on_device(transmission, probe_modes, measured, offset_down, offset_across):
    length = probe_modes.shape[-1]
    scan_count = measured.shape[0]
    rows, cols = lax.axis_size("row"), lax.axis_size("col")
    core = lax.rem(lax.axis_index("col"), 2)
    table = tables(length)

    middle = transmission.shape[1] // 2
    first, rest = lax.optimization_barrier((transmission[:, :middle], transmission))
    last = rest[:, middle:]
    direct = [
        ((row + 1) * cols + col + 1, row * cols + col)
        for row in range(rows - 1)
        for col in range(1, cols - 1, 2)
    ]
    below_first = shifted(first, "row", -1)
    below_last = shifted(last, "row", -1)
    right = shifted(transmission, "col", -1)
    corner_last = lax.ppermute(last, ("row", "col"), direct)
    corner_first = shifted(below_first, "col", -1)
    consts = [table[name] for name in ("right_f", "left_f", "left_b", "right_b", "lane", "sub")]
    picks = [table["pick_rows"], table["pick_cols"]]
    *consts, ordered = prepare(measured, picks, consts)
    relayed = lax.ppermute(below_last, "col", [(col + 1, col) for col in range(0, cols - 1, 2)])

    offsets = (offset_down, offset_across)
    own, to_right, to_below, to_corner, keep, send = process_scans(
        offsets,
        (transmission, right, below_first, below_last, corner_first, corner_last, relayed),
        probe_modes,
        ordered,
        consts,
    )

    keep = keep + swapped(send, "col", 1)
    parts = 2 if cols % 4 == 0 else 1
    groups = chip_groups(parts)
    piece = scatter_sum(keep.reshape((-1, length)), groups)
    piece = sum_over_groups(piece, 2 * parts)
    scans_total = scan_count * rows * cols
    mine = gather_slices(piece * (1.0 / math.sqrt(scans_total)), groups).reshape(keep.shape)
    other = swapped(mine, "col", 1)
    probe_gradient = place_mode(mine, probe_modes.shape[0], 0)
    probe_gradient = place_mode(other, probe_modes.shape[0], 1, probe_gradient)

    relayed = lax.ppermute(to_corner, "col", [(col, col + 1) for col in range(0, cols - 1, 2)])
    to_below = add_tiles(to_below, relayed, out=VMEM(to_below.shape, jnp.float32))
    from_left = shifted(to_right, "col", 1)
    from_above = shifted(to_below, "row", 1)
    from_corner = lax.ppermute(to_corner, ("row", "col"), [(end, start) for start, end in direct])
    tile = jax.ShapeDtypeStruct(own.shape, jnp.float32)
    own = add_tiles(own, from_left, from_above, from_corner, out=tile)
    return own, probe_gradient


def solution(mesh):
    in_specs = (
        P(None, "row", "col"),
        P(),
        P(("row", "col"), None, None),
        P(("row", "col")),
        P(("row", "col")),
    )
    out_specs = (P(None, "row", "col"), P())
    return jax.shard_map(
        on_device, mesh=mesh, in_specs=in_specs, out_specs=out_specs, check_vma=False
    )
```

```python
import functools
import math

import jax
import jax.numpy as jnp
import numpy as np
from jax import lax
from jax.experimental import pallas as pl
from jax.experimental.pallas import tpu as pltpu
from jax.sharding import PartitionSpec as P


VMEM = pltpu.VMEM
SMEM = pltpu.SMEM
PREPARE_VMEM = 8 * 1024 * 1024
PROCESS_VMEM = 20 * 1024 * 1024


def shifted(block, axis, distance):
    count = lax.axis_size(axis)
    route = [(i - distance, i) for i in range(count) if 0 <= i - distance < count]
    return lax.ppermute(block, axis, route)


def swapped(block, axis, mask):
    return lax.ppermute(block, axis, [(i, i ^ mask) for i in range(lax.axis_size(axis))])


def power_of_two(number):
    return number & (number - 1) == 0


def chip_groups(parts):
    rows, cols = lax.axis_size("row"), lax.axis_size("col")
    return [
        [row * cols + first + core + 2 * part for row in range(rows) for part in range(parts)]
        for first in range(0, cols, 2 * parts)
        for core in range(2)
    ]


def scatter_sum(values, groups):
    count = len(groups[0])
    pieces = values.reshape((count, values.shape[0] // count) + values.shape[1:])
    return jnp.sum(
        lax.all_to_all(pieces, ("row", "col"), 0, 0, axis_index_groups=groups), axis=0
    )


def gather_slices(piece, groups):
    copies = jnp.broadcast_to(piece[None], (len(groups[0]),) + piece.shape)
    slices = lax.all_to_all(copies, ("row", "col"), 0, 0, axis_index_groups=groups)
    return slices.reshape((-1,) + piece.shape[1:])


def sum_over_groups(piece, stride):
    count = lax.axis_size("col")
    if power_of_two(count // stride):
        mask = stride
        while mask < count:
            piece = piece + swapped(piece, "col", mask)
            mask *= 2
        return piece
    groups = [list(range(first, count, stride)) for first in range(stride)]
    copies = jnp.broadcast_to(piece[None], (count // stride,) + piece.shape)
    return jnp.sum(lax.all_to_all(copies, "col", 0, 0, axis_index_groups=groups), axis=0)


def split_table(table):
    high = table.astype(jnp.bfloat16)
    low = (table - high.astype(np.float64)).astype(jnp.bfloat16)
    return high, low


def tables(length):
    half = length // 2
    counter = np.arange(half)
    angles = 2.0 * math.pi * (np.outer(counter, counter) % half) / half
    cosines = np.cos(angles) / math.sqrt(length)
    sines = np.sin(angles) / math.sqrt(length)
    forward = np.block([[cosines, -sines], [sines, cosines]])
    backward = np.block([[cosines, sines], [-sines, cosines]])
    result = {}
    for name, table in (("f", forward), ("b", backward)):
        high, low = split_table(table)
        result["right_" + name] = np.concatenate([high, high, low], axis=0)
        high, low = split_table(np.ascontiguousarray(table.T))
        result["left_" + name] = np.concatenate([high, high, low], axis=1)
    turn = 2.0 * math.pi * counter / length
    result["lane"] = np.stack([np.cos(turn), np.sin(turn)]).astype(np.float32)
    across = np.stack([np.cos(turn), np.sin(turn)]).astype(np.float32)
    result["sub"] = np.ascontiguousarray(np.repeat(across[:, :, None], half, axis=2))
    order = np.concatenate([np.arange(0, length, 2), np.arange(1, length, 2)])
    select = np.zeros((length, length), np.float32)
    select[order, np.arange(length)] = 1.0
    result["pick_cols"] = np.concatenate([select] * 3, axis=0).astype(jnp.bfloat16)
    result["pick_rows"] = np.concatenate([select.T] * 3, axis=1).astype(jnp.bfloat16)
    return result


def halves(values):
    high = values.astype(jnp.bfloat16)
    low = (values - high.astype(jnp.float32)).astype(jnp.bfloat16)
    return high, low


def dot(left, right):
    return jnp.dot(left, right, preferred_element_type=jnp.float32)


def thirds(values):
    high = values.astype(jnp.bfloat16)
    rest = values - high.astype(jnp.float32)
    middle = rest.astype(jnp.bfloat16)
    low = (rest - middle.astype(jnp.float32)).astype(jnp.bfloat16)
    return [high, middle, low]


def prepare_kernel(measured_ref, pick_rows_ref, pick_cols_ref, *refs):
    out_ref = refs[-1]
    for source, target in zip(refs[: len(refs) // 2], refs[len(refs) // 2 :]):
        target[...] = source[...]
    scans, length, _ = measured_ref.shape
    half = length // 2
    for which in range(scans):
        rows = dot(pick_rows_ref[...], jnp.concatenate(thirds(measured_ref[which]), axis=0))
        both = dot(jnp.concatenate(thirds(rows), axis=1), pick_cols_ref[...])
        out_ref[which, :, :length] = both[:half]
        out_ref[which, :, length:] = both[half:]


def scan_kernel(
    down_ref,
    across_ref,
    own_ref,
    right_ref,
    below_first_ref,
    below_last_ref,
    corner_first_ref,
    corner_last_ref,
    relayed_ref,
    probe_ref,
    measured_ref,
    right_f_ref,
    left_f_ref,
    left_b_ref,
    right_b_ref,
    lane_ref,
    sub_ref,
    own_out,
    right_out,
    below_out,
    corner_out,
    keep_out,
    send_out,
    wave_ref,
):
    scans = measured_ref.shape[0]
    modes, _, length, _ = probe_ref.shape
    half = length // 2
    core = lax.rem(lax.axis_index("col"), 2)
    row_of = lax.broadcasted_iota(jnp.int32, (length, length), 0)
    col_of = lax.broadcasted_iota(jnp.int32, (length, length), 1)

    def apply_right(parts, table_ref):
        high, low = halves(parts)
        return dot(jnp.concatenate([high, low, high], axis=1), table_ref[...])

    def apply_left(table_ref, parts):
        high, low = halves(parts)
        return dot(table_ref[...], jnp.concatenate([high, low, high], axis=0))

    def lane_turn():
        return lane_ref[0:1, :], lane_ref[1:2, :]

    for which in range(scans):
        down = down_ref[which]
        across = across_ref[which]
        later_row = row_of < down
        later_col = col_of < across
        up = lax.rem(length - down, length)
        back_across = lax.rem(length - across, length)
        patch = []
        for part in range(2):
            below = jnp.concatenate([below_first_ref[part], below_last_ref[part]], axis=0)
            corner_last = corner_last_ref[part] + relayed_ref[part]
            corner = jnp.concatenate([corner_first_ref[part], corner_last], axis=0)
            merged = jnp.where(
                later_row,
                jnp.where(later_col, corner, below),
                jnp.where(later_col, right_ref[part], own_ref[part]),
            )
            patch.append(pltpu.roll(pltpu.roll(merged, up, 0), back_across, 1))
        patch_r, patch_i = patch

        intensity = None
        for step in range(modes):
            mode = step ^ core
            probe_r, probe_i = probe_ref[mode, 0], probe_ref[mode, 1]
            exit_r = probe_r * patch_r - probe_i * patch_i
            exit_i = probe_r * patch_i + probe_i * patch_r
            cos, sin = lane_turn()
            first_r, last_r = exit_r[:, :half], exit_r[:, half:]
            first_i, last_i = exit_i[:, :half], exit_i[:, half:]
            gap_r, gap_i = first_r - last_r, first_i - last_i
            even = jnp.concatenate([first_r + last_r, first_i + last_i], axis=1)
            odd = jnp.concatenate(
                [gap_r * cos + gap_i * sin, gap_i * cos - gap_r * sin], axis=1
            )
            even = apply_right(even, right_f_ref)
            odd = apply_right(odd, right_f_ref)
            cos, sin = sub_ref[0], sub_ref[1]
            sums, turned = [[], []], [[], []]
            for block in (even, odd):
                top_r, low_r = block[:half, :half], block[half:, :half]
                top_i, low_i = block[:half, half:], block[half:, half:]
                gap_r, gap_i = top_r - low_r, top_i - low_i
                sums[0].append(top_r + low_r)
                sums[1].append(top_i + low_i)
                turned[0].append(gap_r * cos + gap_i * sin)
                turned[1].append(gap_i * cos - gap_r * sin)
            stacked = jnp.concatenate(
                [jnp.concatenate(sums[part] + turned[part], axis=1) for part in range(2)], axis=0
            )
            wave = apply_left(left_f_ref, stacked)
            wave_ref[step] = wave
            wave_r, wave_i = wave[:half], wave[half:]
            square = wave_r * wave_r + wave_i * wave_i
            intensity = square if intensity is None else intensity + square
        resid = intensity - measured_ref[which]

        object_r = object_i = None
        for step in range(modes):
            mode = step ^ core
            wave = wave_ref[step]
            weighted = jnp.concatenate([resid * wave[:half], resid * wave[half:]], axis=0)
            rows = apply_left(left_b_ref, weighted)
            cos, sin = sub_ref[0], sub_ref[1]
            cos = jnp.concatenate([cos, cos], axis=1)
            sin = jnp.concatenate([sin, sin], axis=1)
            even_r, odd_r = rows[:half, :length], rows[:half, length:]
            even_i, odd_i = rows[half:, :length], rows[half:, length:]
            turn_r = odd_r * cos - odd_i * sin
            turn_i = odd_i * cos + odd_r * sin
            real = jnp.concatenate([even_r + turn_r, even_r - turn_r], axis=0)
            imag = jnp.concatenate([even_i + turn_i, even_i - turn_i], axis=0)
            even = jnp.concatenate([real[:, :half], imag[:, :half]], axis=1)
            odd = jnp.concatenate([real[:, half:], imag[:, half:]], axis=1)
            even = apply_right(even, right_b_ref)
            odd = apply_right(odd, right_b_ref)
            cos, sin = lane_turn()
            turn_r = odd[:, :half] * cos - odd[:, half:] * sin
            turn_i = odd[:, half:] * cos + odd[:, :half] * sin
            back_r = jnp.concatenate([even[:, :half] + turn_r, even[:, :half] - turn_r], axis=1)
            back_i = jnp.concatenate([even[:, half:] + turn_i, even[:, half:] - turn_i], axis=1)
            probe_out = (keep_out, send_out)[step]
            term_r = patch_r * back_r + patch_i * back_i
            term_i = patch_r * back_i - patch_i * back_r
            if which == 0:
                probe_out[0] = term_r
                probe_out[1] = term_i
            else:
                probe_out[0] = probe_out[0] + term_r
                probe_out[1] = probe_out[1] + term_i
            probe_r, probe_i = probe_ref[mode, 0], probe_ref[mode, 1]
            term_r = probe_r * back_r + probe_i * back_i
            term_i = probe_r * back_i - probe_i * back_r
            object_r = term_r if object_r is None else object_r + term_r
            object_i = term_i if object_i is None else object_i + term_i

        for part, values in ((0, object_r), (1, object_i)):
            placed = pltpu.roll(pltpu.roll(values, down, 0), across, 1)
            upper = jnp.where(later_row, 0.0, placed)
            lower = jnp.where(later_row, placed, 0.0)
            pieces = (
                (own_out, jnp.where(later_col, 0.0, upper)),
                (right_out, jnp.where(later_col, upper, 0.0)),
                (below_out, jnp.where(later_col, 0.0, lower)),
                (corner_out, jnp.where(later_col, lower, 0.0)),
            )
            for out, piece in pieces:
                if which == 0:
                    out[part] = piece
                else:
                    out[part] = out[part] + piece


def in_space(space, *arrays):
    return [pltpu.with_memory_space_constraint(array, space) for array in arrays]


def whole():
    return pl.BlockSpec(memory_space=VMEM)


def prepare(measured, picks, consts):
    scans, length, _ = measured.shape
    shapes = [VMEM(const.shape, const.dtype) for const in consts]
    return pl.pallas_call(
        prepare_kernel,
        out_shape=shapes + [VMEM((scans, length // 2, 2 * length), jnp.float32)],
        in_specs=[whole()] * (3 + len(consts)),
        out_specs=[whole()] * (1 + len(consts)),
        compiler_params=pltpu.CompilerParams(vmem_limit_bytes=PREPARE_VMEM),
        name="prepare",
    )(*in_space(pltpu.HBM, measured, *picks, *consts))


def process_scans(offsets, tiles, probe_modes, measured, consts):
    modes, _, length, _ = probe_modes.shape
    operands = in_space(VMEM, *tiles, probe_modes, measured, *consts)
    results = [tiles[0].shape] * 4 + [probe_modes.shape[1:]] * 2
    return pl.pallas_call(
        scan_kernel,
        out_shape=[VMEM(shape, jnp.float32) for shape in results],
        in_specs=[pl.BlockSpec(memory_space=SMEM)] * 2 + [whole()] * len(operands),
        out_specs=[whole()] * len(results),
        scratch_shapes=[VMEM((modes, length, 2 * length), jnp.float32)],
        compiler_params=pltpu.CompilerParams(vmem_limit_bytes=PROCESS_VMEM),
        name="process_scans",
    )(*in_space(SMEM, *offsets), *operands)


def place_kernel(step, values_ref, *refs):
    out_ref, sem = refs[-2], refs[-1]
    mode = lax.rem(lax.axis_index("col"), 2) ^ step
    copy = pltpu.make_async_copy(values_ref, out_ref.at[mode], sem)
    copy.start()
    copy.wait()


def place_mode(values, modes, step, into=None):
    before = () if into is None else (into,)
    return pl.pallas_call(
        functools.partial(place_kernel, step),
        out_shape=jax.ShapeDtypeStruct((modes,) + values.shape, values.dtype),
        in_specs=[whole()] + [pl.BlockSpec(memory_space=pl.ANY)] * len(before),
        out_specs=pl.BlockSpec(memory_space=pl.ANY),
        scratch_shapes=[pltpu.SemaphoreType.DMA],
        input_output_aliases={1: 0} if before else {},
        compiler_params=pltpu.CompilerParams(vmem_limit_bytes=PREPARE_VMEM),
        name="place_mode",
    )(*in_space(VMEM, values), *before)


def add_kernel(*refs):
    total = refs[0][...]
    for ref in refs[1:-1]:
        total = total + ref[...]
    refs[-1][...] = total


def add_tiles(*tiles, out):
    return pl.pallas_call(
        add_kernel,
        out_shape=out,
        in_specs=[whole()] * len(tiles),
        out_specs=whole(),
        compiler_params=pltpu.CompilerParams(vmem_limit_bytes=PREPARE_VMEM),
        name="add_tiles",
    )(*in_space(VMEM, *tiles))


def on_device(transmission, probe_modes, measured, offset_down, offset_across):
    length = probe_modes.shape[-1]
    scan_count = measured.shape[0]
    rows, cols = lax.axis_size("row"), lax.axis_size("col")
    core = lax.rem(lax.axis_index("col"), 2)
    table = tables(length)

    middle = transmission.shape[1] // 2
    first, rest = lax.optimization_barrier((transmission[:, :middle], transmission))
    last = rest[:, middle:]
    direct = [
        ((row + 1) * cols + col + 1, row * cols + col)
        for row in range(rows - 1)
        for col in range(1, cols - 1, 2)
    ]
    below_first = shifted(first, "row", -1)
    below_last = shifted(last, "row", -1)
    right = shifted(transmission, "col", -1)
    corner_last = lax.ppermute(last, ("row", "col"), direct)
    corner_first = shifted(below_first, "col", -1)
    consts = [table[name] for name in ("right_f", "left_f", "left_b", "right_b", "lane", "sub")]
    picks = [table["pick_rows"], table["pick_cols"]]
    *consts, ordered = prepare(measured, picks, consts)
    relayed = lax.ppermute(below_last, "col", [(col + 1, col) for col in range(0, cols - 1, 2)])

    offsets = (offset_down, offset_across)
    own, to_right, to_below, to_corner, keep, send = process_scans(
        offsets,
        (transmission, right, below_first, below_last, corner_first, corner_last, relayed),
        probe_modes,
        ordered,
        consts,
    )

    keep = keep + swapped(send, "col", 1)
    parts = 2 if cols % 4 == 0 else 1
    groups = chip_groups(parts)
    piece = scatter_sum(keep.reshape((-1, length)), groups)
    piece = sum_over_groups(piece, 2 * parts)
    scans_total = scan_count * rows * cols
    mine = gather_slices(piece * (1.0 / math.sqrt(scans_total)), groups).reshape(keep.shape)
    other = swapped(mine, "col", 1)
    probe_gradient = place_mode(mine, probe_modes.shape[0], 0)
    probe_gradient = place_mode(other, probe_modes.shape[0], 1, probe_gradient)

    def across(cores):
        return [(col, col + 1) for col in range(cores, cols - 1, 2)]

    def downward(cores):
        return [
            (row * cols + col, (row + 1) * cols + col)
            for row in range(rows - 1)
            for col in range(cores, cols, 2)
        ]

    tile = jax.ShapeDtypeStruct(own.shape, jnp.float32)
    on_chip = VMEM(own.shape, jnp.float32)
    relayed = lax.ppermute(to_corner, "col", across(0))
    passed = lax.ppermute(to_corner, "col", across(1))
    to_below_odd = add_tiles(to_below, relayed, out=on_chip)
    above_odd = lax.ppermute(to_below_odd, ("row", "col"), downward(1))
    to_below_even = add_tiles(to_below, passed, out=on_chip)
    above_even = lax.ppermute(to_below_even, ("row", "col"), downward(0))
    from_left = shifted(to_right, "col", 1)
    own = add_tiles(own, from_left, above_odd, above_even, out=tile)
    return own, probe_gradient


def solution(mesh):
    in_specs = (
        P(None, "row", "col"),
        P(),
        P(("row", "col"), None, None),
        P(("row", "col")),
        P(("row", "col")),
    )
    out_specs = (P(None, "row", "col"), P())
    return jax.shard_map(
        on_device, mesh=mesh, in_specs=in_specs, out_specs=out_specs, check_vma=False
    )
```

```python
import functools
import math

import jax
import jax.numpy as jnp
import numpy as np
from jax import lax
from jax.experimental import pallas as pl
from jax.experimental.pallas import tpu as pltpu
from jax.sharding import PartitionSpec as P


VMEM = pltpu.VMEM
SMEM = pltpu.SMEM
PREPARE_VMEM = 8 * 1024 * 1024
PROCESS_VMEM = 20 * 1024 * 1024


def shifted(block, axis, distance):
    count = lax.axis_size(axis)
    route = [(i - distance, i) for i in range(count) if 0 <= i - distance < count]
    return lax.ppermute(block, axis, route)


def swapped(block, axis, mask):
    return lax.ppermute(block, axis, [(i, i ^ mask) for i in range(lax.axis_size(axis))])


def power_of_two(number):
    return number & (number - 1) == 0


def chip_groups(parts):
    rows, cols = lax.axis_size("row"), lax.axis_size("col")
    return [
        [row * cols + first + core + 2 * part for row in range(rows) for part in range(parts)]
        for first in range(0, cols, 2 * parts)
        for core in range(2)
    ]


def scatter_sum(values, groups):
    count = len(groups[0])
    pieces = values.reshape((count, values.shape[0] // count) + values.shape[1:])
    return sum_pieces(lax.all_to_all(pieces, ("row", "col"), 0, 0, axis_index_groups=groups))


def gather_slices(piece, groups):
    copies = jnp.broadcast_to(piece[None], (len(groups[0]),) + piece.shape)
    slices = lax.all_to_all(copies, ("row", "col"), 0, 0, axis_index_groups=groups)
    return slices.reshape((-1,) + piece.shape[1:])


def sum_over_groups(piece, stride):
    count = lax.axis_size("col")
    if power_of_two(count // stride):
        mask = stride
        while mask < count:
            piece = piece + swapped(piece, "col", mask)
            mask *= 2
        return piece
    groups = [list(range(first, count, stride)) for first in range(stride)]
    copies = jnp.broadcast_to(piece[None], (count // stride,) + piece.shape)
    return jnp.sum(lax.all_to_all(copies, "col", 0, 0, axis_index_groups=groups), axis=0)


def split_table(table):
    high = table.astype(jnp.bfloat16)
    low = (table - high.astype(np.float64)).astype(jnp.bfloat16)
    return high, low


def tables(length):
    half = length // 2
    counter = np.arange(half)
    angles = 2.0 * math.pi * (np.outer(counter, counter) % half) / half
    cosines = np.cos(angles) / math.sqrt(length)
    sines = np.sin(angles) / math.sqrt(length)
    forward = np.block([[cosines, -sines], [sines, cosines]])
    backward = np.block([[cosines, sines], [-sines, cosines]])
    result = {}
    for name, table in (("f", forward), ("b", backward)):
        high, low = split_table(table)
        result["right_" + name] = np.concatenate([high, high, low], axis=0)
        high, low = split_table(np.ascontiguousarray(table.T))
        result["left_" + name] = np.concatenate([high, high, low], axis=1)
    turn = 2.0 * math.pi * counter / length
    result["lane"] = np.stack([np.cos(turn), np.sin(turn)]).astype(np.float32)
    across = np.stack([np.cos(turn), np.sin(turn)]).astype(np.float32)
    result["sub"] = np.ascontiguousarray(np.repeat(across[:, :, None], half, axis=2))
    order = np.concatenate([np.arange(0, length, 2), np.arange(1, length, 2)])
    select = np.zeros((length, length), np.float32)
    select[order, np.arange(length)] = 1.0
    result["pick_cols"] = np.concatenate([select] * 3, axis=0).astype(jnp.bfloat16)
    result["pick_rows"] = np.concatenate([select.T] * 3, axis=1).astype(jnp.bfloat16)
    return result


def halves(values):
    high = values.astype(jnp.bfloat16)
    low = (values - high.astype(jnp.float32)).astype(jnp.bfloat16)
    return high, low


def dot(left, right):
    return jnp.dot(left, right, preferred_element_type=jnp.float32)


def thirds(values):
    high = values.astype(jnp.bfloat16)
    rest = values - high.astype(jnp.float32)
    middle = rest.astype(jnp.bfloat16)
    low = (rest - middle.astype(jnp.float32)).astype(jnp.bfloat16)
    return [high, middle, low]


def prepare_kernel(measured_ref, pick_rows_ref, pick_cols_ref, *refs):
    out_ref = refs[-1]
    for source, target in zip(refs[: len(refs) // 2], refs[len(refs) // 2 :]):
        target[...] = source[...]
    scans, length, _ = measured_ref.shape
    half = length // 2
    for which in range(scans):
        rows = dot(pick_rows_ref[...], jnp.concatenate(thirds(measured_ref[which]), axis=0))
        both = dot(jnp.concatenate(thirds(rows), axis=1), pick_cols_ref[...])
        out_ref[which, :, :length] = both[:half]
        out_ref[which, :, length:] = both[half:]


def scan_kernel(
    down_ref,
    across_ref,
    own_ref,
    right_ref,
    below_first_ref,
    below_last_ref,
    corner_first_ref,
    corner_last_ref,
    relayed_ref,
    probe_ref,
    measured_ref,
    right_f_ref,
    left_f_ref,
    left_b_ref,
    right_b_ref,
    lane_ref,
    sub_ref,
    own_out,
    right_out,
    below_out,
    corner_out,
    keep_out,
    send_out,
    wave_ref,
):
    scans = measured_ref.shape[0]
    modes, _, length, _ = probe_ref.shape
    half = length // 2
    core = lax.rem(lax.axis_index("col"), 2)
    row_of = lax.broadcasted_iota(jnp.int32, (length, length), 0)
    col_of = lax.broadcasted_iota(jnp.int32, (length, length), 1)

    def apply_right(parts, table_ref):
        high, low = halves(parts)
        return dot(jnp.concatenate([high, low, high], axis=1), table_ref[...])

    def apply_left(table_ref, parts):
        high, low = halves(parts)
        return dot(table_ref[...], jnp.concatenate([high, low, high], axis=0))

    def lane_turn():
        return lane_ref[0:1, :], lane_ref[1:2, :]

    for which in range(scans):
        down = down_ref[which]
        across = across_ref[which]
        later_row = row_of < down
        later_col = col_of < across
        up = lax.rem(length - down, length)
        back_across = lax.rem(length - across, length)
        patch = []
        for part in range(2):
            below = jnp.concatenate([below_first_ref[part], below_last_ref[part]], axis=0)
            corner_last = corner_last_ref[part] + relayed_ref[part]
            corner = jnp.concatenate([corner_first_ref[part], corner_last], axis=0)
            merged = jnp.where(
                later_row,
                jnp.where(later_col, corner, below),
                jnp.where(later_col, right_ref[part], own_ref[part]),
            )
            patch.append(pltpu.roll(pltpu.roll(merged, up, 0), back_across, 1))
        patch_r, patch_i = patch

        intensity = None
        for step in range(modes):
            mode = step ^ core
            probe_r, probe_i = probe_ref[mode, 0], probe_ref[mode, 1]
            exit_r = probe_r * patch_r - probe_i * patch_i
            exit_i = probe_r * patch_i + probe_i * patch_r
            cos, sin = lane_turn()
            first_r, last_r = exit_r[:, :half], exit_r[:, half:]
            first_i, last_i = exit_i[:, :half], exit_i[:, half:]
            gap_r, gap_i = first_r - last_r, first_i - last_i
            even = jnp.concatenate([first_r + last_r, first_i + last_i], axis=1)
            odd = jnp.concatenate(
                [gap_r * cos + gap_i * sin, gap_i * cos - gap_r * sin], axis=1
            )
            even = apply_right(even, right_f_ref)
            odd = apply_right(odd, right_f_ref)
            cos, sin = sub_ref[0], sub_ref[1]
            sums, turned = [[], []], [[], []]
            for block in (even, odd):
                top_r, low_r = block[:half, :half], block[half:, :half]
                top_i, low_i = block[:half, half:], block[half:, half:]
                gap_r, gap_i = top_r - low_r, top_i - low_i
                sums[0].append(top_r + low_r)
                sums[1].append(top_i + low_i)
                turned[0].append(gap_r * cos + gap_i * sin)
                turned[1].append(gap_i * cos - gap_r * sin)
            stacked = jnp.concatenate(
                [jnp.concatenate(sums[part] + turned[part], axis=1) for part in range(2)], axis=0
            )
            wave = apply_left(left_f_ref, stacked)
            wave_ref[step] = wave
            wave_r, wave_i = wave[:half], wave[half:]
            square = wave_r * wave_r + wave_i * wave_i
            intensity = square if intensity is None else intensity + square
        resid = intensity - measured_ref[which]

        object_r = object_i = None
        for step in range(modes):
            mode = step ^ core
            wave = wave_ref[step]
            weighted = jnp.concatenate([resid * wave[:half], resid * wave[half:]], axis=0)
            rows = apply_left(left_b_ref, weighted)
            cos, sin = sub_ref[0], sub_ref[1]
            cos = jnp.concatenate([cos, cos], axis=1)
            sin = jnp.concatenate([sin, sin], axis=1)
            even_r, odd_r = rows[:half, :length], rows[:half, length:]
            even_i, odd_i = rows[half:, :length], rows[half:, length:]
            turn_r = odd_r * cos - odd_i * sin
            turn_i = odd_i * cos + odd_r * sin
            real = jnp.concatenate([even_r + turn_r, even_r - turn_r], axis=0)
            imag = jnp.concatenate([even_i + turn_i, even_i - turn_i], axis=0)
            even = jnp.concatenate([real[:, :half], imag[:, :half]], axis=1)
            odd = jnp.concatenate([real[:, half:], imag[:, half:]], axis=1)
            even = apply_right(even, right_b_ref)
            odd = apply_right(odd, right_b_ref)
            cos, sin = lane_turn()
            turn_r = odd[:, :half] * cos - odd[:, half:] * sin
            turn_i = odd[:, half:] * cos + odd[:, :half] * sin
            back_r = jnp.concatenate([even[:, :half] + turn_r, even[:, :half] - turn_r], axis=1)
            back_i = jnp.concatenate([even[:, half:] + turn_i, even[:, half:] - turn_i], axis=1)
            probe_out = (keep_out, send_out)[step]
            term_r = patch_r * back_r + patch_i * back_i
            term_i = patch_r * back_i - patch_i * back_r
            if which == 0:
                probe_out[0] = term_r
                probe_out[1] = term_i
            else:
                probe_out[0] = probe_out[0] + term_r
                probe_out[1] = probe_out[1] + term_i
            probe_r, probe_i = probe_ref[mode, 0], probe_ref[mode, 1]
            term_r = probe_r * back_r + probe_i * back_i
            term_i = probe_r * back_i - probe_i * back_r
            object_r = term_r if object_r is None else object_r + term_r
            object_i = term_i if object_i is None else object_i + term_i

        for part, values in ((0, object_r), (1, object_i)):
            placed = pltpu.roll(pltpu.roll(values, down, 0), across, 1)
            upper = jnp.where(later_row, 0.0, placed)
            lower = jnp.where(later_row, placed, 0.0)
            pieces = (
                (own_out, jnp.where(later_col, 0.0, upper)),
                (right_out, jnp.where(later_col, upper, 0.0)),
                (below_out, jnp.where(later_col, 0.0, lower)),
                (corner_out, jnp.where(later_col, lower, 0.0)),
            )
            for out, piece in pieces:
                if which == 0:
                    out[part] = piece
                else:
                    out[part] = out[part] + piece


def in_space(space, *arrays):
    return [pltpu.with_memory_space_constraint(array, space) for array in arrays]


def whole():
    return pl.BlockSpec(memory_space=VMEM)


def prepare(measured, picks, consts):
    scans, length, _ = measured.shape
    shapes = [VMEM(const.shape, const.dtype) for const in consts]
    return pl.pallas_call(
        prepare_kernel,
        out_shape=shapes + [VMEM((scans, length // 2, 2 * length), jnp.float32)],
        in_specs=[whole()] * (3 + len(consts)),
        out_specs=[whole()] * (1 + len(consts)),
        compiler_params=pltpu.CompilerParams(vmem_limit_bytes=PREPARE_VMEM),
        name="prepare",
    )(*in_space(pltpu.HBM, measured, *picks, *consts))


def process_scans(offsets, tiles, probe_modes, measured, consts):
    modes, _, length, _ = probe_modes.shape
    operands = in_space(VMEM, *tiles, probe_modes, measured, *consts)
    results = [tiles[0].shape] * 4 + [probe_modes.shape[1:]] * 2
    return pl.pallas_call(
        scan_kernel,
        out_shape=[VMEM(shape, jnp.float32) for shape in results],
        in_specs=[pl.BlockSpec(memory_space=SMEM)] * 2 + [whole()] * len(operands),
        out_specs=[whole()] * len(results),
        scratch_shapes=[VMEM((modes, length, 2 * length), jnp.float32)],
        compiler_params=pltpu.CompilerParams(vmem_limit_bytes=PROCESS_VMEM),
        name="process_scans",
    )(*in_space(pltpu.HBM, *offsets), *operands)


def sum_kernel(pieces_ref, out_ref):
    out_ref[...] = jnp.sum(pieces_ref[...], axis=0)


def sum_pieces(pieces):
    return pl.pallas_call(
        sum_kernel,
        out_shape=VMEM(pieces.shape[1:], pieces.dtype),
        in_specs=[whole()],
        out_specs=whole(),
        compiler_params=pltpu.CompilerParams(vmem_limit_bytes=PREPARE_VMEM),
        name="sum_pieces",
    )(*in_space(VMEM, pieces))


def place_kernel(step, values_ref, *refs):
    out_ref, sem = refs[-2], refs[-1]
    mode = lax.rem(lax.axis_index("col"), 2) ^ step
    copy = pltpu.make_async_copy(values_ref, out_ref.at[mode], sem)
    copy.start()
    copy.wait()


def place_mode(values, modes, step, into=None):
    before = () if into is None else (into,)
    return pl.pallas_call(
        functools.partial(place_kernel, step),
        out_shape=jax.ShapeDtypeStruct((modes,) + values.shape, values.dtype),
        in_specs=[whole()] + [pl.BlockSpec(memory_space=pl.ANY)] * len(before),
        out_specs=pl.BlockSpec(memory_space=pl.ANY),
        scratch_shapes=[pltpu.SemaphoreType.DMA],
        input_output_aliases={1: 0} if before else {},
        compiler_params=pltpu.CompilerParams(vmem_limit_bytes=PREPARE_VMEM),
        name="place_mode",
    )(*in_space(VMEM, values), *before)


def add_kernel(*refs):
    total = refs[0][...]
    for ref in refs[1:-1]:
        total = total + ref[...]
    refs[-1][...] = total


def add_tiles(*tiles, out):
    return pl.pallas_call(
        add_kernel,
        out_shape=out,
        in_specs=[whole()] * len(tiles),
        out_specs=whole(),
        compiler_params=pltpu.CompilerParams(vmem_limit_bytes=PREPARE_VMEM),
        name="add_tiles",
    )(*in_space(VMEM, *tiles))


def on_device(transmission, probe_modes, measured, offset_down, offset_across):
    length = probe_modes.shape[-1]
    scan_count = measured.shape[0]
    rows, cols = lax.axis_size("row"), lax.axis_size("col")
    core = lax.rem(lax.axis_index("col"), 2)
    table = tables(length)

    middle = transmission.shape[1] // 2
    first, rest = lax.optimization_barrier((transmission[:, :middle], transmission))
    last = rest[:, middle:]
    direct = [
        ((row + 1) * cols + col + 1, row * cols + col)
        for row in range(rows - 1)
        for col in range(1, cols - 1, 2)
    ]
    below_first = shifted(first, "row", -1)
    below_last = shifted(last, "row", -1)
    right = shifted(transmission, "col", -1)
    corner_last = lax.ppermute(last, ("row", "col"), direct)
    corner_first = shifted(below_first, "col", -1)
    consts = [table[name] for name in ("right_f", "left_f", "left_b", "right_b", "lane", "sub")]
    picks = [table["pick_rows"], table["pick_cols"]]
    *consts, ordered = prepare(measured, picks, consts)
    relayed = lax.ppermute(below_last, "col", [(col + 1, col) for col in range(0, cols - 1, 2)])

    offsets = (offset_down, offset_across)
    own, to_right, to_below, to_corner, keep, send = process_scans(
        offsets,
        (transmission, right, below_first, below_last, corner_first, corner_last, relayed),
        probe_modes,
        ordered,
        consts,
    )

    keep = keep + swapped(send, "col", 1)
    parts = 2 if cols % 4 == 0 else 1
    groups = chip_groups(parts)
    piece = scatter_sum(keep.reshape((-1, length)), groups)
    piece = sum_over_groups(piece, 2 * parts)
    scans_total = scan_count * rows * cols
    mine = gather_slices(piece * (1.0 / math.sqrt(scans_total)), groups).reshape(keep.shape)
    other = swapped(mine, "col", 1)
    probe_gradient = place_mode(mine, probe_modes.shape[0], 0)
    probe_gradient = place_mode(other, probe_modes.shape[0], 1, probe_gradient)

    relayed = lax.ppermute(to_corner, "col", [(col, col + 1) for col in range(0, cols - 1, 2)])
    to_below = add_tiles(to_below, relayed, out=VMEM(to_below.shape, jnp.float32))
    from_left = shifted(to_right, "col", 1)
    from_above = shifted(to_below, "row", 1)
    from_corner = lax.ppermute(to_corner, ("row", "col"), [(end, start) for start, end in direct])
    tile = jax.ShapeDtypeStruct(own.shape, jnp.float32)
    own = add_tiles(own, from_left, from_above, from_corner, out=tile)
    return own, probe_gradient


def solution(mesh):
    in_specs = (
        P(None, "row", "col"),
        P(),
        P(("row", "col"), None, None),
        P(("row", "col")),
        P(("row", "col")),
    )
    out_specs = (P(None, "row", "col"), P())
    return jax.shard_map(
        on_device, mesh=mesh, in_specs=in_specs, out_specs=out_specs, check_vma=False
    )
```

```python
import functools
import math

import jax
import jax.numpy as jnp
import numpy as np
from jax import lax
from jax.experimental import pallas as pl
from jax.experimental.pallas import tpu as pltpu
from jax.sharding import PartitionSpec as P


VMEM = pltpu.VMEM
SMEM = pltpu.SMEM
PREPARE_VMEM = 8 * 1024 * 1024
PROCESS_VMEM = 20 * 1024 * 1024


def shifted(block, axis, distance):
    count = lax.axis_size(axis)
    route = [(i - distance, i) for i in range(count) if 0 <= i - distance < count]
    return lax.ppermute(block, axis, route)


def swapped(block, axis, mask):
    return lax.ppermute(block, axis, [(i, i ^ mask) for i in range(lax.axis_size(axis))])


def power_of_two(number):
    return number & (number - 1) == 0


def chip_groups(parts):
    rows, cols = lax.axis_size("row"), lax.axis_size("col")
    return [
        [row * cols + first + core + 2 * part for row in range(rows) for part in range(parts)]
        for first in range(0, cols, 2 * parts)
        for core in range(2)
    ]


def scatter_sum(values, groups):
    count = len(groups[0])
    pieces = values.reshape((count, values.shape[0] // count) + values.shape[1:])
    return sum_pieces(lax.all_to_all(pieces, ("row", "col"), 0, 0, axis_index_groups=groups))


def gather_slices(piece, groups):
    copies = jnp.broadcast_to(piece[None], (len(groups[0]),) + piece.shape)
    slices = lax.all_to_all(copies, ("row", "col"), 0, 0, axis_index_groups=groups)
    return slices.reshape((-1,) + piece.shape[1:])


def sum_over_groups(piece, stride):
    count = lax.axis_size("col")
    if power_of_two(count // stride):
        mask = stride
        while mask < count:
            piece = piece + swapped(piece, "col", mask)
            mask *= 2
        return piece
    groups = [list(range(first, count, stride)) for first in range(stride)]
    copies = jnp.broadcast_to(piece[None], (count // stride,) + piece.shape)
    return jnp.sum(lax.all_to_all(copies, "col", 0, 0, axis_index_groups=groups), axis=0)


def split_table(table):
    high = table.astype(jnp.bfloat16)
    low = (table - high.astype(np.float64)).astype(jnp.bfloat16)
    return high, low


def tables(length):
    half = length // 2
    counter = np.arange(half)
    angles = 2.0 * math.pi * (np.outer(counter, counter) % half) / half
    cosines = np.cos(angles) / math.sqrt(length)
    sines = np.sin(angles) / math.sqrt(length)
    forward = np.block([[cosines, -sines], [sines, cosines]])
    backward = np.block([[cosines, sines], [-sines, cosines]])
    result = {}
    for name, table in (("f", forward), ("b", backward)):
        high, low = split_table(table)
        result["right_" + name] = np.concatenate([high, high, low], axis=0)
        high, low = split_table(np.ascontiguousarray(table.T))
        result["left_" + name] = np.concatenate([high, high, low], axis=1)
    turn = 2.0 * math.pi * counter / length
    result["lane"] = np.stack([np.cos(turn), np.sin(turn)]).astype(np.float32)
    across = np.stack([np.cos(turn), np.sin(turn)]).astype(np.float32)
    result["sub"] = np.ascontiguousarray(np.repeat(across[:, :, None], half, axis=2))
    order = np.concatenate([np.arange(0, length, 2), np.arange(1, length, 2)])
    select = np.zeros((length, length), np.float32)
    select[order, np.arange(length)] = 1.0
    result["pick_cols"] = np.concatenate([select] * 3, axis=0).astype(jnp.bfloat16)
    result["pick_rows"] = np.concatenate([select.T] * 3, axis=1).astype(jnp.bfloat16)
    return result


def halves(values):
    high = values.astype(jnp.bfloat16)
    low = (values - high.astype(jnp.float32)).astype(jnp.bfloat16)
    return high, low


def dot(left, right):
    return jnp.dot(left, right, preferred_element_type=jnp.float32)


def thirds(values):
    high = values.astype(jnp.bfloat16)
    rest = values - high.astype(jnp.float32)
    middle = rest.astype(jnp.bfloat16)
    low = (rest - middle.astype(jnp.float32)).astype(jnp.bfloat16)
    return [high, middle, low]


def prepare_kernel(measured_ref, pick_rows_ref, pick_cols_ref, *refs):
    out_ref = refs[-1]
    for source, target in zip(refs[: len(refs) // 2], refs[len(refs) // 2 :]):
        target[...] = source[...]
    scans, length, _ = measured_ref.shape
    half = length // 2
    for which in range(scans):
        rows = dot(pick_rows_ref[...], jnp.concatenate(thirds(measured_ref[which]), axis=0))
        both = dot(jnp.concatenate(thirds(rows), axis=1), pick_cols_ref[...])
        out_ref[which, :, :length] = both[:half]
        out_ref[which, :, length:] = both[half:]


def scan_kernel(
    down_ref,
    across_ref,
    own_ref,
    right_ref,
    below_first_ref,
    below_last_ref,
    corner_first_ref,
    corner_last_ref,
    probe_ref,
    measured_ref,
    right_f_ref,
    left_f_ref,
    left_b_ref,
    right_b_ref,
    lane_ref,
    sub_ref,
    own_out,
    right_out,
    below_out,
    corner_out,
    keep_out,
    send_out,
    wave_ref,
):
    scans = measured_ref.shape[0]
    modes, _, length, _ = probe_ref.shape
    half = length // 2
    core = lax.rem(lax.axis_index("col"), 2)
    row_of = lax.broadcasted_iota(jnp.int32, (length, length), 0)
    col_of = lax.broadcasted_iota(jnp.int32, (length, length), 1)

    def apply_right(parts, table_ref):
        high, low = halves(parts)
        return dot(jnp.concatenate([high, low, high], axis=1), table_ref[...])

    def apply_left(table_ref, parts):
        high, low = halves(parts)
        return dot(table_ref[...], jnp.concatenate([high, low, high], axis=0))

    def lane_turn():
        return lane_ref[0:1, :], lane_ref[1:2, :]

    for which in range(scans):
        down = down_ref[which]
        across = across_ref[which]
        later_row = row_of < down
        later_col = col_of < across
        up = lax.rem(length - down, length)
        back_across = lax.rem(length - across, length)
        patch = []
        for part in range(2):
            below = jnp.concatenate([below_first_ref[part], below_last_ref[part]], axis=0)
            corner = jnp.concatenate([corner_first_ref[part], corner_last_ref[part]], axis=0)
            merged = jnp.where(
                later_row,
                jnp.where(later_col, corner, below),
                jnp.where(later_col, right_ref[part], own_ref[part]),
            )
            patch.append(pltpu.roll(pltpu.roll(merged, up, 0), back_across, 1))
        patch_r, patch_i = patch

        intensity = None
        for step in range(modes):
            mode = step ^ core
            probe_r, probe_i = probe_ref[mode, 0], probe_ref[mode, 1]
            exit_r = probe_r * patch_r - probe_i * patch_i
            exit_i = probe_r * patch_i + probe_i * patch_r
            cos, sin = lane_turn()
            first_r, last_r = exit_r[:, :half], exit_r[:, half:]
            first_i, last_i = exit_i[:, :half], exit_i[:, half:]
            gap_r, gap_i = first_r - last_r, first_i - last_i
            even = jnp.concatenate([first_r + last_r, first_i + last_i], axis=1)
            odd = jnp.concatenate(
                [gap_r * cos + gap_i * sin, gap_i * cos - gap_r * sin], axis=1
            )
            even = apply_right(even, right_f_ref)
            odd = apply_right(odd, right_f_ref)
            cos, sin = sub_ref[0], sub_ref[1]
            sums, turned = [[], []], [[], []]
            for block in (even, odd):
                top_r, low_r = block[:half, :half], block[half:, :half]
                top_i, low_i = block[:half, half:], block[half:, half:]
                gap_r, gap_i = top_r - low_r, top_i - low_i
                sums[0].append(top_r + low_r)
                sums[1].append(top_i + low_i)
                turned[0].append(gap_r * cos + gap_i * sin)
                turned[1].append(gap_i * cos - gap_r * sin)
            stacked = jnp.concatenate(
                [jnp.concatenate(sums[part] + turned[part], axis=1) for part in range(2)], axis=0
            )
            wave = apply_left(left_f_ref, stacked)
            wave_ref[step] = wave
            wave_r, wave_i = wave[:half], wave[half:]
            square = wave_r * wave_r + wave_i * wave_i
            intensity = square if intensity is None else intensity + square
        resid = intensity - measured_ref[which]

        object_r = object_i = None
        for step in range(modes):
            mode = step ^ core
            wave = wave_ref[step]
            weighted = jnp.concatenate([resid * wave[:half], resid * wave[half:]], axis=0)
            rows = apply_left(left_b_ref, weighted)
            cos, sin = sub_ref[0], sub_ref[1]
            cos = jnp.concatenate([cos, cos], axis=1)
            sin = jnp.concatenate([sin, sin], axis=1)
            even_r, odd_r = rows[:half, :length], rows[:half, length:]
            even_i, odd_i = rows[half:, :length], rows[half:, length:]
            turn_r = odd_r * cos - odd_i * sin
            turn_i = odd_i * cos + odd_r * sin
            real = jnp.concatenate([even_r + turn_r, even_r - turn_r], axis=0)
            imag = jnp.concatenate([even_i + turn_i, even_i - turn_i], axis=0)
            even = jnp.concatenate([real[:, :half], imag[:, :half]], axis=1)
            odd = jnp.concatenate([real[:, half:], imag[:, half:]], axis=1)
            even = apply_right(even, right_b_ref)
            odd = apply_right(odd, right_b_ref)
            cos, sin = lane_turn()
            turn_r = odd[:, :half] * cos - odd[:, half:] * sin
            turn_i = odd[:, half:] * cos + odd[:, :half] * sin
            back_r = jnp.concatenate([even[:, :half] + turn_r, even[:, :half] - turn_r], axis=1)
            back_i = jnp.concatenate([even[:, half:] + turn_i, even[:, half:] - turn_i], axis=1)
            probe_out = (keep_out, send_out)[step]
            term_r = patch_r * back_r + patch_i * back_i
            term_i = patch_r * back_i - patch_i * back_r
            if which == 0:
                probe_out[0] = term_r
                probe_out[1] = term_i
            else:
                probe_out[0] = probe_out[0] + term_r
                probe_out[1] = probe_out[1] + term_i
            probe_r, probe_i = probe_ref[mode, 0], probe_ref[mode, 1]
            term_r = probe_r * back_r + probe_i * back_i
            term_i = probe_r * back_i - probe_i * back_r
            object_r = term_r if object_r is None else object_r + term_r
            object_i = term_i if object_i is None else object_i + term_i

        for part, values in ((0, object_r), (1, object_i)):
            placed = pltpu.roll(pltpu.roll(values, down, 0), across, 1)
            upper = jnp.where(later_row, 0.0, placed)
            lower = jnp.where(later_row, placed, 0.0)
            pieces = (
                (own_out, jnp.where(later_col, 0.0, upper)),
                (right_out, jnp.where(later_col, upper, 0.0)),
                (below_out, jnp.where(later_col, 0.0, lower)),
                (corner_out, jnp.where(later_col, lower, 0.0)),
            )
            for out, piece in pieces:
                if which == 0:
                    out[part] = piece
                else:
                    out[part] = out[part] + piece


def in_space(space, *arrays):
    return [pltpu.with_memory_space_constraint(array, space) for array in arrays]


def whole():
    return pl.BlockSpec(memory_space=VMEM)


def prepare(measured, picks, consts):
    scans, length, _ = measured.shape
    shapes = [VMEM(const.shape, const.dtype) for const in consts]
    return pl.pallas_call(
        prepare_kernel,
        out_shape=shapes + [VMEM((scans, length // 2, 2 * length), jnp.float32)],
        in_specs=[whole()] * (3 + len(consts)),
        out_specs=[whole()] * (1 + len(consts)),
        compiler_params=pltpu.CompilerParams(vmem_limit_bytes=PREPARE_VMEM),
        name="prepare",
    )(*in_space(pltpu.HBM, measured, *picks, *consts))


def process_scans(offsets, tiles, probe_modes, measured, consts):
    modes, _, length, _ = probe_modes.shape
    operands = in_space(VMEM, *tiles, probe_modes, measured, *consts)
    results = [tiles[0].shape] * 4 + [probe_modes.shape[1:]] * 2
    return pl.pallas_call(
        scan_kernel,
        out_shape=[VMEM(shape, jnp.float32) for shape in results],
        in_specs=[pl.BlockSpec(memory_space=SMEM)] * 2 + [whole()] * len(operands),
        out_specs=[whole()] * len(results),
        scratch_shapes=[VMEM((modes, length, 2 * length), jnp.float32)],
        compiler_params=pltpu.CompilerParams(vmem_limit_bytes=PROCESS_VMEM),
        name="process_scans",
    )(*in_space(pltpu.HBM, *offsets), *operands)


def sum_kernel(pieces_ref, out_ref):
    out_ref[...] = jnp.sum(pieces_ref[...], axis=0)


def sum_pieces(pieces):
    return pl.pallas_call(
        sum_kernel,
        out_shape=VMEM(pieces.shape[1:], pieces.dtype),
        in_specs=[whole()],
        out_specs=whole(),
        compiler_params=pltpu.CompilerParams(vmem_limit_bytes=PREPARE_VMEM),
        name="sum_pieces",
    )(*in_space(VMEM, pieces))


def place_kernel(step, values_ref, *refs):
    out_ref, sem = refs[-2], refs[-1]
    mode = lax.rem(lax.axis_index("col"), 2) ^ step
    copy = pltpu.make_async_copy(values_ref, out_ref.at[mode], sem)
    copy.start()
    copy.wait()


def place_mode(values, modes, step, into=None):
    before = () if into is None else (into,)
    return pl.pallas_call(
        functools.partial(place_kernel, step),
        out_shape=jax.ShapeDtypeStruct((modes,) + values.shape, values.dtype),
        in_specs=[whole()] + [pl.BlockSpec(memory_space=pl.ANY)] * len(before),
        out_specs=pl.BlockSpec(memory_space=pl.ANY),
        scratch_shapes=[pltpu.SemaphoreType.DMA],
        input_output_aliases={1: 0} if before else {},
        compiler_params=pltpu.CompilerParams(vmem_limit_bytes=PREPARE_VMEM),
        name="place_mode",
    )(*in_space(VMEM, values), *before)


def add_kernel(*refs):
    total = refs[0][...]
    for ref in refs[1:-1]:
        total = total + ref[...]
    refs[-1][...] = total


def add_tiles(*tiles, out):
    return pl.pallas_call(
        add_kernel,
        out_shape=out,
        in_specs=[whole()] * len(tiles),
        out_specs=whole(),
        compiler_params=pltpu.CompilerParams(vmem_limit_bytes=PREPARE_VMEM),
        name="add_tiles",
    )(*in_space(VMEM, *tiles))


def on_device(transmission, probe_modes, measured, offset_down, offset_across):
    length = probe_modes.shape[-1]
    scan_count = measured.shape[0]
    rows, cols = lax.axis_size("row"), lax.axis_size("col")
    core = lax.rem(lax.axis_index("col"), 2)
    table = tables(length)

    middle = transmission.shape[1] * 9 // 16 // 8 * 8
    first, rest = lax.optimization_barrier((transmission[:, :middle], transmission))
    last = rest[:, middle:]
    diagonal = [
        ((row + 1) * cols + col + 1, row * cols + col)
        for row in range(rows - 1)
        for col in range(cols - 1)
    ]
    direct = [(start, end) for start, end in diagonal if end % cols % 2 == 1]
    below_first = shifted(first, "row", -1)
    below_last = shifted(last, "row", -1)
    right = shifted(transmission, "col", -1)
    corner_last = lax.ppermute(last, ("row", "col"), diagonal)
    corner_first = shifted(below_first, "col", -1)
    consts = [table[name] for name in ("right_f", "left_f", "left_b", "right_b", "lane", "sub")]
    picks = [table["pick_rows"], table["pick_cols"]]
    *consts, ordered = prepare(measured, picks, consts)
    offsets = (offset_down, offset_across)
    own, to_right, to_below, to_corner, keep, send = process_scans(
        offsets,
        (transmission, right, below_first, below_last, corner_first, corner_last),
        probe_modes,
        ordered,
        consts,
    )

    keep = keep + swapped(send, "col", 1)
    parts = 2 if cols % 4 == 0 else 1
    groups = chip_groups(parts)
    piece = scatter_sum(keep.reshape((-1, length)), groups)
    piece = sum_over_groups(piece, 2 * parts)
    scans_total = scan_count * rows * cols
    mine = gather_slices(piece * (1.0 / math.sqrt(scans_total)), groups).reshape(keep.shape)
    other = swapped(mine, "col", 1)
    probe_gradient = place_mode(mine, probe_modes.shape[0], 0)
    probe_gradient = place_mode(other, probe_modes.shape[0], 1, probe_gradient)

    relayed = lax.ppermute(to_corner, "col", [(col, col + 1) for col in range(0, cols - 1, 2)])
    to_below = add_tiles(to_below, relayed, out=VMEM(to_below.shape, jnp.float32))
    from_left = shifted(to_right, "col", 1)
    from_above = shifted(to_below, "row", 1)
    from_corner = lax.ppermute(to_corner, ("row", "col"), [(end, start) for start, end in direct])
    tile = jax.ShapeDtypeStruct(own.shape, jnp.float32)
    own = add_tiles(own, from_left, from_above, from_corner, out=tile)
    return own, probe_gradient


def solution(mesh):
    in_specs = (
        P(None, "row", "col"),
        P(),
        P(("row", "col"), None, None),
        P(("row", "col")),
        P(("row", "col")),
    )
    out_specs = (P(None, "row", "col"), P())
    return jax.shard_map(
        on_device, mesh=mesh, in_specs=in_specs, out_specs=out_specs, check_vma=False
    )
```

```python
import functools
import math

import jax
import jax.numpy as jnp
import numpy as np
from jax import lax
from jax.experimental import pallas as pl
from jax.experimental.pallas import tpu as pltpu
from jax.sharding import PartitionSpec as P


VMEM = pltpu.VMEM
SMEM = pltpu.SMEM
PREPARE_VMEM = 8 * 1024 * 1024
PROCESS_VMEM = 20 * 1024 * 1024


def shifted(block, axis, distance):
    count = lax.axis_size(axis)
    route = [(i - distance, i) for i in range(count) if 0 <= i - distance < count]
    return lax.ppermute(block, axis, route)


def swapped(block, axis, mask):
    return lax.ppermute(block, axis, [(i, i ^ mask) for i in range(lax.axis_size(axis))])


def power_of_two(number):
    return number & (number - 1) == 0


def chip_groups(parts):
    rows, cols = lax.axis_size("row"), lax.axis_size("col")
    return [
        [row * cols + first + core + 2 * part for row in range(rows) for part in range(parts)]
        for first in range(0, cols, 2 * parts)
        for core in range(2)
    ]


def scatter_sum(values, groups):
    count = len(groups[0])
    pieces = values.reshape((count, values.shape[0] // count) + values.shape[1:])
    return sum_pieces(lax.all_to_all(pieces, ("row", "col"), 0, 0, axis_index_groups=groups))


def gather_slices(piece, groups):
    copies = jnp.broadcast_to(piece[None], (len(groups[0]),) + piece.shape)
    slices = lax.all_to_all(copies, ("row", "col"), 0, 0, axis_index_groups=groups)
    return slices.reshape((-1,) + piece.shape[1:])


def sum_over_groups(piece, stride):
    count = lax.axis_size("col")
    if power_of_two(count // stride):
        mask = stride
        while mask < count:
            piece = piece + swapped(piece, "col", mask)
            mask *= 2
        return piece
    groups = [list(range(first, count, stride)) for first in range(stride)]
    copies = jnp.broadcast_to(piece[None], (count // stride,) + piece.shape)
    return jnp.sum(lax.all_to_all(copies, "col", 0, 0, axis_index_groups=groups), axis=0)


def split_table(table):
    high = table.astype(jnp.bfloat16)
    low = (table - high.astype(np.float64)).astype(jnp.bfloat16)
    return high, low


def tables(length):
    half = length // 2
    counter = np.arange(half)
    angles = 2.0 * math.pi * (np.outer(counter, counter) % half) / half
    cosines = np.cos(angles) / math.sqrt(length)
    sines = np.sin(angles) / math.sqrt(length)
    forward = np.block([[cosines, -sines], [sines, cosines]])
    backward = np.block([[cosines, sines], [-sines, cosines]])
    result = {}
    for name, table in (("f", forward), ("b", backward)):
        high, low = split_table(table)
        result["right_" + name] = np.concatenate([high, high, low], axis=0)
        high, low = split_table(np.ascontiguousarray(table.T))
        result["left_" + name] = np.concatenate([high, high, low], axis=1)
    turn = 2.0 * math.pi * counter / length
    result["lane"] = np.stack([np.cos(turn), np.sin(turn)]).astype(np.float32)
    across = np.stack([np.cos(turn), np.sin(turn)]).astype(np.float32)
    result["sub"] = np.ascontiguousarray(np.repeat(across[:, :, None], half, axis=2))
    order = np.concatenate([np.arange(0, length, 2), np.arange(1, length, 2)])
    select = np.zeros((length, length), np.float32)
    select[order, np.arange(length)] = 1.0
    result["pick_cols"] = np.concatenate([select] * 3, axis=0).astype(jnp.bfloat16)
    result["pick_rows"] = np.concatenate([select.T] * 3, axis=1).astype(jnp.bfloat16)
    return result


def halves(values):
    high = values.astype(jnp.bfloat16)
    low = (values - high.astype(jnp.float32)).astype(jnp.bfloat16)
    return high, low


def dot(left, right):
    return jnp.dot(left, right, preferred_element_type=jnp.float32)


def thirds(values):
    high = values.astype(jnp.bfloat16)
    rest = values - high.astype(jnp.float32)
    middle = rest.astype(jnp.bfloat16)
    low = (rest - middle.astype(jnp.float32)).astype(jnp.bfloat16)
    return [high, middle, low]


def prepare_kernel(measured_ref, pick_rows_ref, pick_cols_ref, *refs):
    out_ref = refs[-1]
    for source, target in zip(refs[: len(refs) // 2], refs[len(refs) // 2 :]):
        target[...] = source[...]
    scans, length, _ = measured_ref.shape
    half = length // 2
    for which in range(scans):
        rows = dot(pick_rows_ref[...], jnp.concatenate(thirds(measured_ref[which]), axis=0))
        both = dot(jnp.concatenate(thirds(rows), axis=1), pick_cols_ref[...])
        out_ref[which, :, :length] = both[:half]
        out_ref[which, :, length:] = both[half:]


def scan_kernel(
    down_ref,
    across_ref,
    own_ref,
    right_ref,
    below_first_ref,
    below_last_ref,
    corner_first_ref,
    corner_last_ref,
    probe_ref,
    measured_ref,
    right_f_ref,
    left_f_ref,
    left_b_ref,
    right_b_ref,
    lane_ref,
    sub_ref,
    own_out,
    right_out,
    below_out,
    corner_out,
    again_out,
    keep_out,
    send_out,
    wave_ref,
):
    scans = measured_ref.shape[0]
    modes, _, length, _ = probe_ref.shape
    half = length // 2
    core = lax.rem(lax.axis_index("col"), 2)
    row_of = lax.broadcasted_iota(jnp.int32, (length, length), 0)
    col_of = lax.broadcasted_iota(jnp.int32, (length, length), 1)

    def apply_right(parts, table_ref):
        high, low = halves(parts)
        return dot(jnp.concatenate([high, low, high], axis=1), table_ref[...])

    def apply_left(table_ref, parts):
        high, low = halves(parts)
        return dot(table_ref[...], jnp.concatenate([high, low, high], axis=0))

    def lane_turn():
        return lane_ref[0:1, :], lane_ref[1:2, :]

    for which in range(scans):
        down = down_ref[which]
        across = across_ref[which]
        later_row = row_of < down
        later_col = col_of < across
        up = lax.rem(length - down, length)
        back_across = lax.rem(length - across, length)
        patch = []
        for part in range(2):
            below = jnp.concatenate([below_first_ref[part], below_last_ref[part]], axis=0)
            corner = jnp.concatenate([corner_first_ref[part], corner_last_ref[part]], axis=0)
            merged = jnp.where(
                later_row,
                jnp.where(later_col, corner, below),
                jnp.where(later_col, right_ref[part], own_ref[part]),
            )
            patch.append(pltpu.roll(pltpu.roll(merged, up, 0), back_across, 1))
        patch_r, patch_i = patch

        intensity = None
        for step in range(modes):
            mode = step ^ core
            probe_r, probe_i = probe_ref[mode, 0], probe_ref[mode, 1]
            exit_r = probe_r * patch_r - probe_i * patch_i
            exit_i = probe_r * patch_i + probe_i * patch_r
            cos, sin = lane_turn()
            first_r, last_r = exit_r[:, :half], exit_r[:, half:]
            first_i, last_i = exit_i[:, :half], exit_i[:, half:]
            gap_r, gap_i = first_r - last_r, first_i - last_i
            even = jnp.concatenate([first_r + last_r, first_i + last_i], axis=1)
            odd = jnp.concatenate(
                [gap_r * cos + gap_i * sin, gap_i * cos - gap_r * sin], axis=1
            )
            even = apply_right(even, right_f_ref)
            odd = apply_right(odd, right_f_ref)
            cos, sin = sub_ref[0], sub_ref[1]
            sums, turned = [[], []], [[], []]
            for block in (even, odd):
                top_r, low_r = block[:half, :half], block[half:, :half]
                top_i, low_i = block[:half, half:], block[half:, half:]
                gap_r, gap_i = top_r - low_r, top_i - low_i
                sums[0].append(top_r + low_r)
                sums[1].append(top_i + low_i)
                turned[0].append(gap_r * cos + gap_i * sin)
                turned[1].append(gap_i * cos - gap_r * sin)
            stacked = jnp.concatenate(
                [jnp.concatenate(sums[part] + turned[part], axis=1) for part in range(2)], axis=0
            )
            wave = apply_left(left_f_ref, stacked)
            wave_ref[step] = wave
            wave_r, wave_i = wave[:half], wave[half:]
            square = wave_r * wave_r + wave_i * wave_i
            intensity = square if intensity is None else intensity + square
        resid = intensity - measured_ref[which]

        object_r = object_i = None
        for step in range(modes):
            mode = step ^ core
            wave = wave_ref[step]
            weighted = jnp.concatenate([resid * wave[:half], resid * wave[half:]], axis=0)
            rows = apply_left(left_b_ref, weighted)
            cos, sin = sub_ref[0], sub_ref[1]
            cos = jnp.concatenate([cos, cos], axis=1)
            sin = jnp.concatenate([sin, sin], axis=1)
            even_r, odd_r = rows[:half, :length], rows[:half, length:]
            even_i, odd_i = rows[half:, :length], rows[half:, length:]
            turn_r = odd_r * cos - odd_i * sin
            turn_i = odd_i * cos + odd_r * sin
            real = jnp.concatenate([even_r + turn_r, even_r - turn_r], axis=0)
            imag = jnp.concatenate([even_i + turn_i, even_i - turn_i], axis=0)
            even = jnp.concatenate([real[:, :half], imag[:, :half]], axis=1)
            odd = jnp.concatenate([real[:, half:], imag[:, half:]], axis=1)
            even = apply_right(even, right_b_ref)
            odd = apply_right(odd, right_b_ref)
            cos, sin = lane_turn()
            turn_r = odd[:, :half] * cos - odd[:, half:] * sin
            turn_i = odd[:, half:] * cos + odd[:, :half] * sin
            back_r = jnp.concatenate([even[:, :half] + turn_r, even[:, :half] - turn_r], axis=1)
            back_i = jnp.concatenate([even[:, half:] + turn_i, even[:, half:] - turn_i], axis=1)
            probe_out = (keep_out, send_out)[step]
            term_r = patch_r * back_r + patch_i * back_i
            term_i = patch_r * back_i - patch_i * back_r
            if which == 0:
                probe_out[0] = term_r
                probe_out[1] = term_i
            else:
                probe_out[0] = probe_out[0] + term_r
                probe_out[1] = probe_out[1] + term_i
            probe_r, probe_i = probe_ref[mode, 0], probe_ref[mode, 1]
            term_r = probe_r * back_r + probe_i * back_i
            term_i = probe_r * back_i - probe_i * back_r
            object_r = term_r if object_r is None else object_r + term_r
            object_i = term_i if object_i is None else object_i + term_i

        for part, values in ((0, object_r), (1, object_i)):
            placed = pltpu.roll(pltpu.roll(values, down, 0), across, 1)
            upper = jnp.where(later_row, 0.0, placed)
            lower = jnp.where(later_row, placed, 0.0)
            pieces = (
                (own_out, jnp.where(later_col, 0.0, upper)),
                (right_out, jnp.where(later_col, upper, 0.0)),
                (below_out, jnp.where(later_col, 0.0, lower)),
                (corner_out, jnp.where(later_col, lower, 0.0)),
            )
            for out, piece in pieces:
                if which == 0:
                    out[part] = piece
                else:
                    out[part] = out[part] + piece
        if which == scans - 1:
            again_out[...] = corner_out[...]


def in_space(space, *arrays):
    return [pltpu.with_memory_space_constraint(array, space) for array in arrays]


def whole():
    return pl.BlockSpec(memory_space=VMEM)


def prepare(measured, picks, consts):
    scans, length, _ = measured.shape
    shapes = [VMEM(const.shape, const.dtype) for const in consts]
    return pl.pallas_call(
        prepare_kernel,
        out_shape=shapes + [VMEM((scans, length // 2, 2 * length), jnp.float32)],
        in_specs=[whole()] * (3 + len(consts)),
        out_specs=[whole()] * (1 + len(consts)),
        compiler_params=pltpu.CompilerParams(vmem_limit_bytes=PREPARE_VMEM),
        name="prepare",
    )(*in_space(pltpu.HBM, measured, *picks, *consts))


def process_scans(offsets, tiles, probe_modes, measured, consts):
    modes, _, length, _ = probe_modes.shape
    operands = in_space(VMEM, *tiles, probe_modes, measured, *consts)
    results = [tiles[0].shape] * 5 + [probe_modes.shape[1:]] * 2
    return pl.pallas_call(
        scan_kernel,
        out_shape=[VMEM(shape, jnp.float32) for shape in results],
        in_specs=[pl.BlockSpec(memory_space=SMEM)] * 2 + [whole()] * len(operands),
        out_specs=[whole()] * len(results),
        scratch_shapes=[VMEM((modes, length, 2 * length), jnp.float32)],
        compiler_params=pltpu.CompilerParams(vmem_limit_bytes=PROCESS_VMEM),
        name="process_scans",
    )(*in_space(pltpu.HBM, *offsets), *operands)


def sum_kernel(pieces_ref, out_ref):
    out_ref[...] = jnp.sum(pieces_ref[...], axis=0)


def sum_pieces(pieces):
    return pl.pallas_call(
        sum_kernel,
        out_shape=VMEM(pieces.shape[1:], pieces.dtype),
        in_specs=[whole()],
        out_specs=whole(),
        compiler_params=pltpu.CompilerParams(vmem_limit_bytes=PREPARE_VMEM),
        name="sum_pieces",
    )(*in_space(VMEM, pieces))


def place_kernel(step, values_ref, *refs):
    out_ref, sem = refs[-2], refs[-1]
    mode = lax.rem(lax.axis_index("col"), 2) ^ step
    copy = pltpu.make_async_copy(values_ref, out_ref.at[mode], sem)
    copy.start()
    copy.wait()


def place_mode(values, modes, step, into=None):
    before = () if into is None else (into,)
    return pl.pallas_call(
        functools.partial(place_kernel, step),
        out_shape=jax.ShapeDtypeStruct((modes,) + values.shape, values.dtype),
        in_specs=[whole()] + [pl.BlockSpec(memory_space=pl.ANY)] * len(before),
        out_specs=pl.BlockSpec(memory_space=pl.ANY),
        scratch_shapes=[pltpu.SemaphoreType.DMA],
        input_output_aliases={1: 0} if before else {},
        compiler_params=pltpu.CompilerParams(vmem_limit_bytes=PREPARE_VMEM),
        name="place_mode",
    )(*in_space(VMEM, values), *before)


def add_kernel(*refs):
    total = refs[0][...]
    for ref in refs[1:-1]:
        total = total + ref[...]
    refs[-1][...] = total


def add_tiles(*tiles, out):
    return pl.pallas_call(
        add_kernel,
        out_shape=out,
        in_specs=[whole()] * len(tiles),
        out_specs=whole(),
        compiler_params=pltpu.CompilerParams(vmem_limit_bytes=PREPARE_VMEM),
        name="add_tiles",
    )(*in_space(VMEM, *tiles))


def on_device(transmission, probe_modes, measured, offset_down, offset_across):
    length = probe_modes.shape[-1]
    scan_count = measured.shape[0]
    rows, cols = lax.axis_size("row"), lax.axis_size("col")
    core = lax.rem(lax.axis_index("col"), 2)
    table = tables(length)

    middle = transmission.shape[1] * 9 // 16 // 8 * 8
    first, rest = lax.optimization_barrier((transmission[:, :middle], transmission))
    last = rest[:, middle:]
    diagonal = [
        ((row + 1) * cols + col + 1, row * cols + col)
        for row in range(rows - 1)
        for col in range(cols - 1)
    ]
    direct = [(start, end) for start, end in diagonal if end % cols % 2 == 1]
    below_first = shifted(first, "row", -1)
    below_last = shifted(last, "row", -1)
    right = shifted(transmission, "col", -1)
    corner_last = lax.ppermute(last, ("row", "col"), diagonal)
    corner_first = shifted(below_first, "col", -1)
    consts = [table[name] for name in ("right_f", "left_f", "left_b", "right_b", "lane", "sub")]
    picks = [table["pick_rows"], table["pick_cols"]]
    *consts, ordered = prepare(measured, picks, consts)
    offsets = (offset_down, offset_across)
    own, to_right, to_below, to_corner, to_corner_again, keep, send = process_scans(
        offsets,
        (transmission, right, below_first, below_last, corner_first, corner_last),
        probe_modes,
        ordered,
        consts,
    )

    keep = keep + swapped(send, "col", 1)
    parts = 2 if cols % 4 == 0 else 1
    groups = chip_groups(parts)
    piece = scatter_sum(keep.reshape((-1, length)), groups)
    piece = sum_over_groups(piece, 2 * parts)
    scans_total = scan_count * rows * cols
    mine = gather_slices(piece * (1.0 / math.sqrt(scans_total)), groups).reshape(keep.shape)
    other = swapped(mine, "col", 1)
    probe_gradient = place_mode(mine, probe_modes.shape[0], 0)
    probe_gradient = place_mode(other, probe_modes.shape[0], 1, probe_gradient)

    relayed = lax.ppermute(to_corner, "col", [(col, col + 1) for col in range(0, cols - 1, 2)])
    to_below = add_tiles(to_below, relayed, out=VMEM(to_below.shape, jnp.float32))
    from_left = shifted(to_right, "col", 1)
    from_above = shifted(to_below, "row", 1)
    from_corner = lax.ppermute(to_corner_again, ("row", "col"), [(end, start) for start, end in direct])
    tile = jax.ShapeDtypeStruct(own.shape, jnp.float32)
    own = add_tiles(own, from_left, from_above, from_corner, out=tile)
    return own, probe_gradient


def solution(mesh):
    in_specs = (
        P(None, "row", "col"),
        P(),
        P(("row", "col"), None, None),
        P(("row", "col")),
        P(("row", "col")),
    )
    out_specs = (P(None, "row", "col"), P())
    return jax.shard_map(
        on_device, mesh=mesh, in_specs=in_specs, out_specs=out_specs, check_vma=False
    )
```
